32 devices in a mesh: exp: 4 (over z), tile: 8 (over y, x, core).
Axes of the slice: x: 2, y: 2, z: 4, core: 2. Of those that a mesh axis runs over, the one named last changes fastest.
Arguments:
- science: bfloat16 [4, 8, 128, 256], P('exp', 'tile'), may hold values from -6 to 6
- mask_bits: int32 [4, 8, 128, 256], P('exp', 'tile'), may hold values from 0 to 1023, as said below
- variance: bfloat16 [4, 8, 128, 256], P('exp', 'tile'), may hold values from 0.25 to 4
- kernel_poly: float32 [4, 8, 8, 3], P('exp', 'tile'), may hold values from -5 to 5
- basis_rows: bfloat16 [8, 31], replicated, may hold values from -1 to 1
- basis_cols: bfloat16 [8, 31], replicated, may hold values from -1 to 1
- destination: int32 [4, 8, 16, 1], P('exp', 'tile'), may hold values from 0 to 7, as said below
- row_offset: int32 [4, 8, 16], P('exp', 'tile'), may hold values from 0 to 1023, as said below
Outputs:
- template: bfloat16 [8192, 128], P('tile')
- difference: bfloat16 [4, 8, 128, 256], P('exp', 'tile')
The draws below stay inside these ranges and needn't reach their ends.
Inputs may be any that keep to these rules, and one draw needn't show every extreme that they name: `destination`: the pieces of the CCD region at tile index t land, in order of piece number, in contiguous runs on tiles t, t + 1 and t + 2 modulo 8; at most 8 pieces of one region land in one tile, and in every draw some region has exactly 8 in one tile. `row_offset`: offsets of consecutive rows of pieces mostly rise by about 16, wrapping within a tile. `mask_bits`: A pixel is rejected where any of bits 0, 1 or 2 is set; only bits 0 to 9 are used, and in every draw some pixel has all ten set.
All inputs are finite; a program needn't handle non-finite values.
Results may differ from the reference program's by a relative error of at most 0.0063.
Values may be sent and summed in bfloat16 or wider, within the bound.
No kernel may reach another device: no remote copies, remote signals or barrier semaphores. Data moves between devices by JAX's collectives and lax.ppermute only.
A program may use at most 64 MiB of HBM per device.

```python
import math
import jax
import jax.numpy as jnp
from jax import lax

ROWS = 128
COLS = 256
PR = 16
PC = 128
TR = 1024
KS = 31
NB = 8
PIECES = 16
N_EXP = 4
N_TILE = 8


def draw_mask_bits(key, part):
    grid_shape = (N_EXP, N_TILE, ROWS, COLS)
    bit_total = jnp.zeros(grid_shape, jnp.int32)
    for bit_number in range(10):
        dice_rolls = jax.random.randint(jax.random.fold_in(key, bit_number + 11), grid_shape, 0, 25)
        bit_total = bit_total + jnp.where(dice_rolls == 0, 2 ** bit_number, 0).astype(jnp.int32)
    cell_total = N_EXP * N_TILE * ROWS * COLS
    chosen_cell = jax.random.randint(jax.random.fold_in(key, 97), (), 0, cell_total)
    cell_number = jnp.arange(cell_total, dtype=jnp.int32).reshape(grid_shape)
    return jnp.where(cell_number == chosen_cell, 1023, bit_total).astype(jnp.int32)


def draw_destination(key, part):
    slot_most = PIECES // 2
    start_shift = jax.random.randint(jax.random.fold_in(key, 5), (N_EXP, N_TILE, 1), 0, slot_most)
    piece_number = jnp.arange(PIECES, dtype=jnp.int32)[None, None, :]
    step_over = (piece_number + start_shift) // slot_most
    tile_number = jnp.arange(N_TILE, dtype=jnp.int32)[None, :, None]
    return ((tile_number + step_over) % N_TILE)[..., None].astype(jnp.int32)


def draw_row_offset(key, part):
    block_cols = COLS // PC
    base_row = jax.random.randint(jax.random.fold_in(key, 7), (N_EXP, N_TILE, 1), 0, TR)
    jitter = jax.random.randint(jax.random.fold_in(key, 8), (N_EXP, N_TILE, PIECES), 0, PR)
    row_block = (jnp.arange(PIECES, dtype=jnp.int32) // block_cols)[None, None, :]
    return ((base_row + PR * row_block + jitter) % TR).astype(jnp.int32)


def levels(stream_key, shape, shards, smallest, high):
    gain = 1.0
    for axis_at, shards_of in shards:
        draws = jax.random.uniform(jax.random.fold_in(jax.random.fold_in(stream_key, 6), axis_at), (shards_of,), jnp.float32, smallest / len(shards), high / len(shards))
        gain = gain * jnp.repeat(jnp.exp(draws), shape[axis_at] // shards_of).reshape((-1,) + (1,) * (len(shape) - 1 - axis_at))
    return gain


def centred(rng, shape, deviation, reach, cuts=(), kind=jnp.bfloat16):
    values = jax.random.normal(rng, shape, jnp.float32) * deviation
    if len(cuts) > 0:
        values = levels(rng, shape, cuts, -0.22, 0.18) * values
    return jnp.clip(values, min=-reach, max=reach).astype(kind)


def setup_inputs(seed: int = 0) -> dict:
    key_of = jax.random.split(jax.random.key(seed), 9)
    return {
        "science": centred(key_of[0], (N_EXP, N_TILE, ROWS, COLS), 1.0, 6.0, ((0, 4), (1, 8))),
        "mask_bits": draw_mask_bits(jax.random.fold_in(key_of[8], 71), 0),
        "variance": jnp.clip(jnp.exp(math.log(4.0) - 2.7725887 * jax.random.uniform(key_of[2], (N_EXP, N_TILE, ROWS, COLS), jnp.float32) ** levels(key_of[2], (N_EXP, N_TILE, ROWS, COLS), ((0, 4), (1, 8)), -0.2, 0.2)), 0.25, 4.0).astype(jnp.bfloat16),
        "kernel_poly": centred(key_of[3], (N_EXP, N_TILE, NB, 3), 0.35, 5.0, ((0, 4), (1, 8)), jnp.float32),
        "basis_rows": centred(key_of[4], (NB, KS), KS ** -0.5, 1.0),
        "basis_cols": centred(key_of[5], (NB, KS), KS ** -0.5, 1.0),
        "destination": draw_destination(jax.random.fold_in(key_of[8], 71), 0),
        "row_offset": draw_row_offset(jax.random.fold_in(key_of[8], 71), 0),
    }


def toeplitz(kernel_taps, length):
    half_width = kernel_taps.shape[1] // 2
    position = jnp.arange(length, dtype=jnp.int32)
    offset_index = position[:, None] - position[None, :] + half_width
    inside = (offset_index >= 0) & (offset_index < kernel_taps.shape[1])
    tap_index = jnp.where(inside, offset_index, 0).astype(jnp.int32)
    band_table = jnp.take(kernel_taps, tap_index, axis=1)
    return jnp.where(inside[None], band_table, jnp.zeros_like(band_table))


def coefficient_maps(kernel_terms, height, across):
    y_norm = (jnp.arange(height, dtype=jnp.int32).astype(jnp.float32) - (height - 1) / 2.0) / (height / 2.0)
    x_norm = (jnp.arange(across, dtype=jnp.int32).astype(jnp.float32) - (across - 1) / 2.0) / (across / 2.0)
    term_values = kernel_terms.astype(jnp.float32)
    return (term_values[:, 0, None, None] + term_values[:, 1, None, None] * y_norm[None, :, None]
            + term_values[:, 2, None, None] * x_norm[None, None, :])


def match_kernel(region, kernel_terms, basis_rows, basis_cols):
    height, across = region.shape
    col_band = toeplitz(basis_cols, across).astype(jnp.float32)
    row_band = toeplitz(basis_rows, height).astype(jnp.float32)
    first_pass = jnp.einsum('yc,bcx->byx', region.astype(jnp.float32), col_band).astype(jnp.bfloat16)
    first_pass = lax.optimization_barrier(first_pass)
    second_pass = jnp.einsum('biy,bix->byx', row_band, first_pass.astype(jnp.float32))
    return jnp.sum(coefficient_maps(kernel_terms, height, across) * second_pass, axis=0)


def reference(science, mask_bits, variance, kernel_poly, basis_rows, basis_cols, destination, row_offset):
    devices_all = N_EXP * N_TILE
    regions = science.reshape(devices_all, ROWS, COLS)
    terms_all = kernel_poly.reshape(devices_all, NB, 3)

    def match_pair(pair_args):
        return match_kernel(pair_args[0], pair_args[1], basis_rows, basis_cols)

    matched = lax.map(match_pair, (regions, terms_all))
    rejected = jnp.bitwise_and(mask_bits.reshape(devices_all, ROWS, COLS), 7) != 0
    weight = jnp.where(rejected, jnp.float32(0.0), 1.0 / variance.reshape(devices_all, ROWS, COLS).astype(jnp.float32))
    weighted = (matched * weight).astype(jnp.bfloat16)
    weight_sent = weight.astype(jnp.bfloat16)

    def to_pieces(picture):
        return picture.reshape(devices_all, ROWS // PR, PR, COLS // PC, PC).transpose(0, 1, 3, 2, 4).reshape(-1, PR, PC)

    target = destination.reshape(devices_all, PIECES).astype(jnp.int32)
    offset = row_offset.reshape(devices_all, PIECES).astype(jnp.int32)
    offset = jnp.where(target == N_TILE - 1, jnp.minimum(offset, TR - PR), offset)
    sky_start = (target * TR + offset).reshape(-1).astype(jnp.int32)
    sky_index = (sky_start[:, None] + jnp.arange(PR, dtype=jnp.int32)[None, :]).reshape(-1)
    sky_sum = jnp.zeros((N_TILE * TR, PC), jnp.float32).at[sky_index].add(
        to_pieces(weighted).reshape(-1, PC).astype(jnp.float32))
    sky_weight = jnp.zeros((N_TILE * TR, PC), jnp.float32).at[sky_index].add(
        to_pieces(weight_sent).reshape(-1, PC).astype(jnp.float32))
    template = (sky_sum / jnp.maximum(sky_weight, 1.0)).astype(jnp.bfloat16)
    cutout = template[sky_index]
    back_image = cutout.reshape(devices_all, ROWS // PR, COLS // PC, PR, PC).transpose(0, 1, 3, 2, 4).reshape(devices_all, ROWS, COLS)
    difference = (matched - back_image.astype(jnp.float32)).astype(jnp.bfloat16)
    return template, difference.reshape(N_EXP, N_TILE, ROWS, COLS)
```

```python
import jax
import jax.numpy as jnp
from jax import lax
from jax.experimental import pallas as pl
from jax.experimental.pallas import tpu as pltpu
from jax.sharding import PartitionSpec as P

PR = 16
PC = 128
TR = 1024
F32 = jnp.float32
BF16 = jnp.bfloat16
SENT = 32.0
REACH = 3
PARAMS = pltpu.CompilerParams(vmem_limit_bytes=24 * 1024 * 1024)


def iota(shape, dim):
    return lax.broadcasted_iota(jnp.int32, shape, dim)


def dot(a, b, ca=1, cb=0):
    return lax.dot_general(a, b, (((ca,), (cb,)), ((), ())), preferred_element_type=F32)


def circulant(taps, reverse):
    count, ks = taps.shape
    half = ks // 2
    tap, lane = iota((ks, PC), 0), iota((ks, PC), 1)
    place = (half - tap) if reverse else (tap - half)
    pick = jnp.where((place + PC) % PC == lane, 1.0, 0.0).astype(BF16)
    row = dot(taps, pick)
    return [
        pltpu.roll(jnp.broadcast_to(row[b : b + 1], (PC, PC)), 0, 1, stride=1, stride_axis=0)
        for b in range(count)
    ]


def shares(exps):
    return PC // exps, PC // 4


def piece_scalars(dest_ref, off_ref, p, tile, tiles):
    target = dest_ref[p]
    offset = off_ref[p]
    offset = jnp.where(target == tiles - 1, jnp.minimum(offset, TR - PR), offset)
    return (target - tile + tiles) % tiles, offset


def match_body(
    exps, tiles, sci_ref, mask_ref, var_ref, poly_ref, brow_ref, bcol_ref, dest_ref, off_ref,
    matched_ref, *z_refs,
):
    exp, tile = lax.axis_index("exp"), lax.axis_index("tile")
    height, across = sci_ref.shape
    bases = brow_ref.shape[0]
    d = iota((PC, PC), 1) - iota((PC, PC), 0)
    zero = jnp.zeros((PC, PC), F32)
    cols = circulant(bcol_ref[...], True)
    rows = circulant(brow_ref[...], False)
    sci = sci_ref[...]
    y = (iota((height, across), 0).astype(F32) - (height - 1) / 2.0) / (height / 2.0)
    x = (iota((height, across), 1).astype(F32) - (across - 1) / 2.0) / (across / 2.0)
    matched = jnp.zeros((height, across), F32)
    for b in range(bases):
        mid = jnp.where(jnp.abs(d) < PC // 2, cols[b], zero)
        up = jnp.where(d < -(PC // 2), cols[b], zero)
        low = jnp.where(d > PC // 2, cols[b], zero)
        band = jnp.concatenate(
            [jnp.concatenate([mid, up], 1), jnp.concatenate([low, mid], 1)], 0
        ).astype(BF16)
        first = dot(sci, band).astype(BF16)
        row_band = jnp.where(jnp.abs(d) < PC // 2, rows[b], zero).astype(BF16)
        second = dot(row_band, first)
        matched += (poly_ref[b, 0] + poly_ref[b, 1] * y + poly_ref[b, 2] * x) * second
    matched_ref[...] = matched
    rejected = jnp.bitwise_and(mask_ref[...], 7) != 0
    weight = jnp.where(rejected, 0.0, 1.0 / var_ref[...].astype(F32))
    weighted = matched * weight
    parts = [weighted[:, :PC], weighted[:, PC:], weight[:, :PC], weight[:, PC:]]
    share, span = shares(exps)
    group = iota((height, PC), 1) // span

    lane = iota((1, PC), 1)
    meta = jnp.zeros((PR, PC), F32)
    sub = iota((PR, PC), 0)
    for c in range(2):
        pos = jnp.zeros((1, PC), jnp.int32)
        step = jnp.zeros((1, PC), jnp.int32)
        for rb in range(height // PR):
            rel, offset = piece_scalars(dest_ref, off_ref, 2 * rb + c, tile, tiles)
            here = lane // PR == rb
            pos = jnp.where(here, offset + lane % PR, pos)
            step = jnp.where(here, rel, step)
        for i, v in enumerate((pos // 32, pos % 32, step)):
            meta = jnp.where(sub == 3 * c + i, v.astype(F32), meta)
    meta = meta.astype(BF16)
    for k in range(exps):
        j = jnp.bitwise_xor(exp, k)
        out = jnp.zeros((height, PC), F32)
        for g in range(4):
            moved = pltpu.roll(parts[g], (PC + span * g - share * j) % PC, 1)
            out = jnp.where(group == g, moved, out)
        z_refs[k][0:height] = out.astype(BF16)
        z_refs[k][height : height + PR] = meta


def pick_body(exps, *refs):
    z_refs, (m1_ref, m2_ref, m3_ref) = refs[:exps], refs[exps:]
    height = z_refs[0].shape[0] - PR
    half = height // 2
    _, span = shares(exps)
    lanes = iota((height, PC), 1)
    odd = (lanes // span) % 2 == 1
    sub16, lane16 = iota((PR, PC), 0), iota((PR, PC), 1)
    to_cols = jnp.where(sub16 == 2 + 3 * ((lane16 // span) % 2), 1.0, 0.0).astype(BF16)
    spill_row = iota((REACH * PR, PC), 0)
    spill = jnp.zeros((REACH * PR, PC), F32)
    metas1 = [jnp.zeros((PR, PC), F32) for _ in range(meta_tiles(exps))]
    metas2 = [jnp.zeros((PR, PC), F32) for _ in range(meta_tiles(exps))]
    first_half = iota((1, PC), 1) < half
    for k in range(exps):
        data = z_refs[k][0:height]
        meta = z_refs[k][height : height + PR]
        step_at = dot(meta, to_cols, 0, 0)
        top, bottom = data[:half], data[half:]
        m1_ref[half * k : half * (k + 1)] = jnp.where(step_at[:half] == 1.0, top, bottom)
        m2_ref[half * k : half * (k + 1)] = bottom
        meta = meta.astype(F32)
        sums = []
        for c in range(2):
            hi, lo, step = (meta[3 * c + i : 3 * c + i + 1] for i in range(3))
            over = hi * 32.0 + lo - TR
            at = jnp.where(over >= 0.0, over + PR * step, -1.0).astype(jnp.int32)
            sums.append(dot(jnp.where(spill_row == at, 1.0, 0.0).astype(BF16), data))
            hi1 = jnp.where(step == 1.0, hi, -SENT)
            hi2 = jnp.where(step == 2.0, hi, -SENT)
            swapped = [pltpu.roll(v, half, 1) for v in (hi1, lo, hi2, lo)]
            use_top = step == 1.0
            hi_1 = jnp.where(use_top, hi1, swapped[0])
            lo_1 = jnp.where(use_top, lo, swapped[1])
            hi_2, lo_2 = swapped[2], swapped[3]
            if k % 2 == 1:
                hi_1, lo_1 = pltpu.roll(hi_1, half, 1), pltpu.roll(lo_1, half, 1)
                hi_2, lo_2 = hi2, lo
            keep = first_half if k % 2 == 0 else jnp.logical_not(first_half)
            row = 4 * (k // 2) + 2 * c
            tile_at, row = row // PR, row % PR
            for metas, values in ((metas1, (hi_1, lo_1)), (metas2, (hi_2, lo_2))):
                for i, v in enumerate(values):
                    metas[tile_at] = jnp.where((sub16 == row + i) & keep, v, metas[tile_at])
        spill += jnp.where((iota((REACH * PR, PC), 1) // span) % 2 == 1, sums[1], sums[0])
    coarse = spill.astype(BF16)
    fine = (spill - coarse.astype(F32)).astype(BF16)
    base = half * exps
    for ref, metas, s in ((m1_ref, metas1, 0), (m2_ref, metas2, 1)):
        for i, m in enumerate(metas):
            ref[base + PR * i : base + PR * (i + 1)] = m.astype(BF16)
        at = base + PR * len(metas)
        ref[at : at + PR] = coarse[PR * s : PR * (s + 1)]
        ref[at + PR : at + 2 * PR] = fine[PR * s : PR * (s + 1)]
    m3_ref[0:PR] = coarse[2 * PR :]
    m3_ref[PR : 2 * PR] = fine[2 * PR :]


def meta_tiles(exps):
    return -(-2 * exps // PR)


def sum_body(exps, *refs):
    z_refs, (m1_ref, m2_ref, m3_ref, out_ref) = refs[:exps], refs[exps:]
    height = z_refs[0].shape[0] - PR
    half = height // 2
    share, span = shares(exps)
    base = half * exps
    tiles = meta_tiles(exps)
    first_half = iota((1, PC), 1) < half
    data = []
    places = ([], [])
    for p in range(exps // 2):
        data += [z_refs[2 * p][0:half], z_refs[2 * p + 1][0:half]]
        metas = [z_refs[2 * p + i][height : height + PR].astype(F32) for i in range(2)]
        for c in range(2):
            pos = []
            for m in metas:
                hi, lo, step = (m[3 * c + i : 3 * c + i + 1] for i in range(3))
                pos.append(jnp.where(step == 0.0, hi * 32.0 + lo, -1.0))
            places[c].append(jnp.where(first_half, pos[0], pltpu.roll(pos[1], half, 1)))
    for ref in (m1_ref, m2_ref):
        data.append(ref[0:base])
        for p in range(exps // 2):
            tile_at, row = 4 * p // PR, 4 * p % PR
            m = ref[base + PR * tile_at : base + PR * (tile_at + 1)].astype(F32)
            for c in range(2):
                at = row + 2 * c
                places[c].append(m[at : at + 1] * 32.0 + m[at + 1 : at + 2])
    data = jnp.concatenate(data, 0)
    at = base + PR * tiles
    spill = jnp.zeros((PR, PC), F32)
    for ref, start in ((m1_ref, at), (m2_ref, at), (m3_ref, 0)):
        for i in range(2):
            spill += ref[start + PR * i : start + PR * (i + 1)].astype(F32)
    rows = TR // exps
    group = iota((rows, PC), 1) // span
    owned = iota((rows, PC), 1) // share
    packed = jnp.zeros((rows, PC), F32)
    places = [[v.astype(jnp.int32) for v in vs] for vs in places]
    for q in range(exps):
        row = iota((rows, PC), 0) + rows * q
        both = []
        for c in range(2):
            hot = jnp.concatenate(
                [jnp.where(row == v, 1.0, 0.0).astype(BF16) for v in places[c]], 1
            )
            both.append(dot(hot, data))
        total = jnp.where(group % 2 == 1, both[1], both[0])
        if q == 0:
            total = jnp.concatenate([total[:PR] + spill, total[PR:]], 0)
        total += pltpu.roll(total, PC - span, 1)
        quotient = total / jnp.maximum(pltpu.roll(total, PC - 2 * span, 1), 1.0)
        if q:
            quotient = pltpu.roll(quotient, share * q, 1)
        packed = jnp.where(owned == q, quotient, packed)
    out_ref[...] = packed.astype(BF16)


def cut_body(exps, *refs):
    packed_refs = refs[:exps]
    z_ref, m1_ref, m2_ref = refs[exps : exps + 3]
    template_ref, own_ref, n1_ref, n2_ref, n3_ref = refs[exps + 3 :]
    exp = lax.axis_index("exp")
    height = z_ref.shape[0] - PR
    half = height // 2
    share, _ = shares(exps)
    base = half * exps
    rows = TR // exps
    lane = iota((rows, PC), 1) // share
    packed = [r[...].astype(F32) for r in packed_refs]
    blocks = []
    for q in range(exps):
        block = jnp.zeros((rows, PC), F32)
        for k in range(exps):
            j = jnp.bitwise_xor(exp, k)
            moved = pltpu.roll(packed[k], (PC + share * (j - q)) % PC, 1)
            block = jnp.where(lane == j, moved, block)
        blocks.append(block.astype(BF16))
    template = jnp.concatenate(blocks, 0)
    template_ref[...] = template
    sub16 = iota((PR, PC), 0)
    hots = []
    for ref, at, first, invalid in (
        (z_ref, height, (0, 3), True), (m1_ref, base, (0, 2), False), (m2_ref, base, (0, 2), False),
    ):
        meta = ref[at : at + PR]
        for c in range(2):
            scale = jnp.where(sub16 == first[c], 32.0, jnp.where(sub16 == first[c] + 1, 1.0, 0.0))
            if invalid:
                scale = jnp.where(sub16 == 3 * c + 2, -2.0 * TR, scale)
            pos = dot(meta, scale.astype(BF16), 0, 0)[:half].astype(jnp.int32)
            lanes = iota((half, PC), 1)
            hots.append(
                jnp.concatenate(
                    [
                        jnp.where(lanes + PC * i == pos, 1.0, 0.0).astype(BF16)
                        for i in range(TR // PC)
                    ],
                    1,
                )
            )
    cut = dot(jnp.concatenate(hots, 0), template).astype(BF16)
    head = template[:PR]
    own_ref[...] = cut[:height]
    n1_ref[0:height] = cut[height : 2 * height]
    n1_ref[height : height + PR] = head
    n2_ref[0:height] = cut[2 * height :]
    n2_ref[height : height + PR] = head
    n3_ref[...] = head


def subtract_body(tiles, matched_ref, own_ref, n1_ref, n2_ref, n3_ref, dest_ref, off_ref, out_ref):
    tile = lax.axis_index("tile")
    height = own_ref.shape[0]
    half = height // 2
    lane = iota((PR, PC), 1)
    sub = iota((PR, PC), 0)
    heads = [n1_ref[height : height + PR], n2_ref[height : height + PR], n3_ref[...]]
    heads.append(jnp.zeros((PC - REACH * PR, PC), BF16))
    heads = jnp.concatenate(heads, 0)
    for c in range(2):
        hots, backs = [], []
        for rb in range(height // PR):
            rel, offset = piece_scalars(dest_ref, off_ref, 2 * rb + c, tile, tiles)
            at = half * c + (PR * rb) % half
            middle = n1_ref[at : at + PR].astype(F32)
            if PR * rb < half:
                backs.append(jnp.where(rel == 0, own_ref[at : at + PR].astype(F32), middle))
            else:
                backs.append(jnp.where(rel == 2, n2_ref[at : at + PR].astype(F32), middle))
            over = sub + (offset - TR)
            hots.append(jnp.where((over >= 0) & (lane == over + PR * rel), 1.0, 0.0).astype(BF16))
        back = jnp.concatenate(backs, 0) + dot(jnp.concatenate(hots, 0), heads)
        out_ref[:, PC * c : PC * (c + 1)] = (matched_ref[:, PC * c : PC * (c + 1)] - back).astype(BF16)


VM = pl.BlockSpec(memory_space=pltpu.VMEM)
SM = pl.BlockSpec(memory_space=pltpu.SMEM)


def call(body, outs, specs, name):
    return pl.pallas_call(
        body,
        out_shape=tuple(jax.ShapeDtypeStruct(s, t) for s, t in outs),
        in_specs=specs,
        out_specs=tuple(VM for _ in outs),
        compiler_params=PARAMS,
        name=name,
    )


def along_exp(x, k, exps):
    return lax.ppermute(x, "exp", [(i, i ^ k) for i in range(exps)])


def along_tile(x, by, tiles):
    return lax.ppermute(x, "tile", [(i, (i + by) % tiles) for i in range(tiles)])


def program_of(exps, tiles):
    def body(science, mask_bits, variance, kernel_poly, basis_rows, basis_cols, destination, row_offset):
        height, across = science.shape[2:]
        bases = basis_rows.shape[0]
        half = height // 2
        dest, off = destination.reshape(-1), row_offset.reshape(-1)
        message = ((height + PR, PC), BF16)
        matched, *z = call(
            lambda *r: match_body(exps, tiles, *r),
            [((height, across), F32)] + [message] * exps,
            [VM, VM, VM, SM, VM, VM, SM, SM],
            "match",
        )(
            science.reshape(height, across), mask_bits.reshape(height, across),
            variance.reshape(height, across), kernel_poly.reshape(bases, 3),
            basis_rows, basis_cols, dest, off,
        )
        z = [z[0]] + [along_exp(z[k], k, exps) for k in range(1, exps)]
        big = ((half * exps + PR * meta_tiles(exps) + 2 * PR, PC), BF16)
        m1, m2, m3 = call(
            lambda *r: pick_body(exps, *r), [big, big, ((2 * PR, PC), BF16)], [VM] * exps, "pick"
        )(*z)
        m1, m2, m3 = (along_tile(m, i + 1, tiles) for i, m in enumerate((m1, m2, m3)))
        (packed,) = call(
            lambda *r: sum_body(exps, *r), [((TR // exps, PC), BF16)], [VM] * (exps + 3), "sum"
        )(*z, m1, m2, m3)
        all_packed = [packed] + [along_exp(packed, k, exps) for k in range(1, exps)]
        template, own, n1, n2, n3 = call(
            lambda *r: cut_body(exps, *r),
            [((TR, PC), BF16), ((height, PC), BF16), message, message, ((PR, PC), BF16)],
            [VM] * (exps + 3),
            "cut",
        )(*all_packed, z[0], m1, m2)
        n1, n2, n3 = (along_tile(n, -1 - i, tiles) for i, n in enumerate((n1, n2, n3)))
        (difference,) = call(
            lambda *r: subtract_body(tiles, *r), [((height, across), BF16)],
            [VM] * 5 + [SM] * 2, "subtract",
        )(matched, own, n1, n2, n3, dest, off)
        return template, difference[None, None]

    return body


def solution(mesh):
    placed = (
        P("exp", "tile", None, None),
        P("exp", "tile", None, None),
        P("exp", "tile", None, None),
        P("exp", "tile", None, None),
        P(),
        P(),
        P("exp", "tile", None, None),
        P("exp", "tile", None),
    )
    return jax.shard_map(
        program_of(mesh.shape["exp"], mesh.shape["tile"]),
        mesh=mesh,
        in_specs=placed,
        out_specs=(P("tile", None), P("exp", "tile", None, None)),
        check_vma=False,
    )
```

```python
import jax
import jax.numpy as jnp
from jax import lax
from jax.experimental import pallas as pl
from jax.experimental.pallas import tpu as pltpu
from jax.sharding import PartitionSpec as P

PR = 16
PC = 128
TR = 1024
F32 = jnp.float32
BF16 = jnp.bfloat16
SENT = 32.0
REACH = 3
PARAMS = pltpu.CompilerParams(vmem_limit_bytes=24 * 1024 * 1024)


def iota(shape, dim):
    return lax.broadcasted_iota(jnp.int32, shape, dim)


def dot(a, b, ca=1, cb=0):
    return lax.dot_general(a, b, (((ca,), (cb,)), ((), ())), preferred_element_type=F32)


def circulant(taps, reverse):
    count, ks = taps.shape
    half = ks // 2
    tap, lane = iota((ks, PC), 0), iota((ks, PC), 1)
    place = (half - tap) if reverse else (tap - half)
    pick = jnp.where((place + PC) % PC == lane, 1.0, 0.0).astype(BF16)
    row = dot(taps, pick)
    return [
        pltpu.roll(jnp.broadcast_to(row[b : b + 1], (PC, PC)), 0, 1, stride=1, stride_axis=0)
        for b in range(count)
    ]


def shares(exps):
    return PC // exps, PC // 4


def piece_scalars(dest_ref, off_ref, p, tile, tiles):
    target = dest_ref[p]
    offset = off_ref[p]
    offset = jnp.where(target == tiles - 1, jnp.minimum(offset, TR - PR), offset)
    return (target - tile + tiles) % tiles, offset


def match_body(exps, tiles, *refs):
    args, matched_ref, z_refs = refs[:8], refs[8], refs[9 : 9 + exps]
    held, sems = refs[9 + exps : 17 + exps], refs[17 + exps]
    copies = [pltpu.make_async_copy(a, h, sems.at[i]) for i, (a, h) in enumerate(zip(args, held))]
    for copy in copies:
        copy.start()
    brow_ref, bcol_ref, sci_ref, poly_ref, mask_ref, var_ref, dest_ref, off_ref = held
    exp, tile = lax.axis_index("exp"), lax.axis_index("tile")
    height, across = sci_ref.shape
    bases = brow_ref.shape[0]
    copies[0].wait()
    copies[1].wait()
    d = iota((PC, PC), 1) - iota((PC, PC), 0)
    zero = jnp.zeros((PC, PC), F32)
    cols = circulant(bcol_ref[...], True)
    rows = circulant(brow_ref[...], False)
    copies[2].wait()
    copies[3].wait()
    sci = sci_ref[...]
    y = (iota((height, across), 0).astype(F32) - (height - 1) / 2.0) / (height / 2.0)
    x = (iota((height, across), 1).astype(F32) - (across - 1) / 2.0) / (across / 2.0)
    matched = jnp.zeros((height, across), F32)
    for b in range(bases):
        mid = jnp.where(jnp.abs(d) < PC // 2, cols[b], zero)
        up = jnp.where(d < -(PC // 2), cols[b], zero)
        low = jnp.where(d > PC // 2, cols[b], zero)
        band = jnp.concatenate(
            [jnp.concatenate([mid, up], 1), jnp.concatenate([low, mid], 1)], 0
        ).astype(BF16)
        first = dot(sci, band).astype(BF16)
        row_band = jnp.where(jnp.abs(d) < PC // 2, rows[b], zero).astype(BF16)
        second = dot(row_band, first)
        matched += (poly_ref[0, 0, 0, b] + poly_ref[0, 1, 0, b] * y + poly_ref[0, 2, 0, b] * x) * second
    matched_ref[...] = matched
    for copy in copies[4:]:
        copy.wait()
    rejected = jnp.bitwise_and(mask_ref[...], 7) != 0
    weight = jnp.where(rejected, 0.0, 1.0 / var_ref[...].astype(F32))
    weighted = matched * weight
    parts = [weighted[:, :PC], weighted[:, PC:], weight[:, :PC], weight[:, PC:]]
    share, span = shares(exps)
    group = iota((height, PC), 1) // span

    lane = iota((1, PC), 1)
    meta = jnp.zeros((PR, PC), F32)
    sub = iota((PR, PC), 0)
    for c in range(2):
        pos = jnp.zeros((1, PC), jnp.int32)
        step = jnp.zeros((1, PC), jnp.int32)
        for rb in range(height // PR):
            rel, offset = piece_scalars(dest_ref, off_ref, 2 * rb + c, tile, tiles)
            here = lane // PR == rb
            pos = jnp.where(here, offset + lane % PR, pos)
            step = jnp.where(here, rel, step)
        for i, v in enumerate((pos // 32, pos % 32, step)):
            meta = jnp.where(sub == 3 * c + i, v.astype(F32), meta)
    meta = meta.astype(BF16)
    for k in range(exps):
        j = jnp.bitwise_xor(exp, k)
        out = jnp.zeros((height, PC), F32)
        for g in range(4):
            moved = pltpu.roll(parts[g], (PC + span * g - share * j) % PC, 1)
            out = jnp.where(group == g, moved, out)
        z_refs[k][0:height] = out.astype(BF16)
        z_refs[k][height : height + PR] = meta


def pick_body(exps, *refs):
    z_refs, (m1_ref, m2_ref, m3_ref) = refs[:exps], refs[exps:]
    height = z_refs[0].shape[0] - PR
    half = height // 2
    _, span = shares(exps)
    lanes = iota((height, PC), 1)
    odd = (lanes // span) % 2 == 1
    sub16, lane16 = iota((PR, PC), 0), iota((PR, PC), 1)
    to_cols = jnp.where(sub16 == 2 + 3 * ((lane16 // span) % 2), 1.0, 0.0).astype(BF16)
    spill_row = iota((REACH * PR, PC), 0)
    spill = jnp.zeros((REACH * PR, PC), F32)
    metas1 = [jnp.zeros((PR, PC), F32) for _ in range(meta_tiles(exps))]
    metas2 = [jnp.zeros((PR, PC), F32) for _ in range(meta_tiles(exps))]
    first_half = iota((1, PC), 1) < half
    for k in range(exps):
        data = z_refs[k][0:height]
        meta = z_refs[k][height : height + PR]
        step_at = dot(meta, to_cols, 0, 0)
        top, bottom = data[:half], data[half:]
        m1_ref[half * k : half * (k + 1)] = jnp.where(step_at[:half] == 1.0, top, bottom)
        m2_ref[half * k : half * (k + 1)] = bottom
        meta = meta.astype(F32)
        sums = []
        for c in range(2):
            hi, lo, step = (meta[3 * c + i : 3 * c + i + 1] for i in range(3))
            over = hi * 32.0 + lo - TR
            at = jnp.where(over >= 0.0, over + PR * step, -1.0).astype(jnp.int32)
            sums.append(dot(jnp.where(spill_row == at, 1.0, 0.0).astype(BF16), data))
            hi1 = jnp.where(step == 1.0, hi, -SENT)
            hi2 = jnp.where(step == 2.0, hi, -SENT)
            swapped = [pltpu.roll(v, half, 1) for v in (hi1, lo, hi2, lo)]
            use_top = step == 1.0
            hi_1 = jnp.where(use_top, hi1, swapped[0])
            lo_1 = jnp.where(use_top, lo, swapped[1])
            hi_2, lo_2 = swapped[2], swapped[3]
            if k % 2 == 1:
                hi_1, lo_1 = pltpu.roll(hi_1, half, 1), pltpu.roll(lo_1, half, 1)
                hi_2, lo_2 = hi2, lo
            keep = first_half if k % 2 == 0 else jnp.logical_not(first_half)
            row = 4 * (k // 2) + 2 * c
            tile_at, row = row // PR, row % PR
            for metas, values in ((metas1, (hi_1, lo_1)), (metas2, (hi_2, lo_2))):
                for i, v in enumerate(values):
                    metas[tile_at] = jnp.where((sub16 == row + i) & keep, v, metas[tile_at])
        spill += jnp.where((iota((REACH * PR, PC), 1) // span) % 2 == 1, sums[1], sums[0])
    coarse = spill.astype(BF16)
    fine = (spill - coarse.astype(F32)).astype(BF16)
    base = half * exps
    for ref, metas, s in ((m1_ref, metas1, 0), (m2_ref, metas2, 1)):
        for i, m in enumerate(metas):
            ref[base + PR * i : base + PR * (i + 1)] = m.astype(BF16)
        at = base + PR * len(metas)
        ref[at : at + PR] = coarse[PR * s : PR * (s + 1)]
        ref[at + PR : at + 2 * PR] = fine[PR * s : PR * (s + 1)]
    m3_ref[0:PR] = coarse[2 * PR :]
    m3_ref[PR : 2 * PR] = fine[2 * PR :]


def meta_tiles(exps):
    return -(-2 * exps // PR)


def hot_sums(places, data, row_count, q):
    row = iota((row_count, PC), 0) + row_count * q
    return [
        dot(jnp.concatenate([jnp.where(row == v, 1.0, 0.0).astype(BF16) for v in vs], 1), data)
        for vs in places
    ]


def own_body(exps, *refs):
    z_refs, out_ref = refs[:exps], refs[exps]
    height = z_refs[0].shape[0] - PR
    half = height // 2
    _, span = shares(exps)
    first_half = iota((1, PC), 1) < half
    data = []
    places = ([], [])
    for p in range(exps // 2):
        data += [z_refs[2 * p][0:half], z_refs[2 * p + 1][0:half]]
        metas = [z_refs[2 * p + i][height : height + PR].astype(F32) for i in range(2)]
        for c in range(2):
            pos = []
            for m in metas:
                hi, lo, step = (m[3 * c + i : 3 * c + i + 1] for i in range(3))
                pos.append(jnp.where(step == 0.0, hi * 32.0 + lo, -1.0))
            pos = jnp.where(first_half, pos[0], pltpu.roll(pos[1], half, 1))
            places[c].append(pos.astype(jnp.int32))
    data = jnp.concatenate(data, 0)
    rows = TR // exps
    odd = (iota((rows, PC), 1) // span) % 2 == 1
    for q in range(exps):
        both = hot_sums(places, data, rows, q)
        out_ref[rows * q : rows * (q + 1)] = jnp.where(odd, both[1], both[0])


def sum_body(exps, own_ref, m1_ref, m2_ref, m3_ref, out_ref):
    share, span = shares(exps)
    tiles = meta_tiles(exps)
    base = m1_ref.shape[0] - PR * tiles - 2 * PR
    data = []
    places = ([], [])
    for ref in (m1_ref, m2_ref):
        data.append(ref[0:base])
        for p in range(exps // 2):
            tile_at, row = 4 * p // PR, 4 * p % PR
            m = ref[base + PR * tile_at : base + PR * (tile_at + 1)].astype(F32)
            for c in range(2):
                at = row + 2 * c
                places[c].append((m[at : at + 1] * 32.0 + m[at + 1 : at + 2]).astype(jnp.int32))
    data = jnp.concatenate(data, 0)
    at = base + PR * tiles
    spill = jnp.zeros((PR, PC), F32)
    for ref, start in ((m1_ref, at), (m2_ref, at), (m3_ref, 0)):
        for i in range(2):
            spill += ref[start + PR * i : start + PR * (i + 1)].astype(F32)
    rows = TR // exps
    group = iota((rows, PC), 1) // span
    owned = iota((rows, PC), 1) // share
    packed = jnp.zeros((rows, PC), F32)
    for q in range(exps):
        both = hot_sums(places, data, rows, q)
        total = jnp.where(group % 2 == 1, both[1], both[0]) + own_ref[rows * q : rows * (q + 1)]
        if q == 0:
            total = jnp.concatenate([total[:PR] + spill, total[PR:]], 0)
        total += pltpu.roll(total, PC - span, 1)
        quotient = total / jnp.maximum(pltpu.roll(total, PC - 2 * span, 1), 1.0)
        if q:
            quotient = pltpu.roll(quotient, share * q, 1)
        packed = jnp.where(owned == q, quotient, packed)
    out_ref[...] = packed.astype(BF16)


def unpack(exps, packed_refs):
    exp = lax.axis_index("exp")
    share, _ = shares(exps)
    rows = TR // exps
    lane = iota((rows, PC), 1) // share
    packed = [r[...].astype(F32) for r in packed_refs]
    blocks = []
    for q in range(exps):
        block = jnp.zeros((rows, PC), F32)
        for k in range(exps):
            j = jnp.bitwise_xor(exp, k)
            moved = pltpu.roll(packed[k], (PC + share * (j - q)) % PC, 1)
            block = jnp.where(lane == j, moved, block)
        blocks.append(block.astype(BF16))
    return blocks


def template_body(exps, *refs):
    rows = TR // exps
    for q, block in enumerate(unpack(exps, refs[:exps])):
        refs[exps][rows * q : rows * (q + 1)] = block


def cut_body(exps, *refs):
    template = jnp.concatenate(unpack(exps, refs[:exps]), 0)
    z_ref, m1_ref, m2_ref = refs[exps : exps + 3]
    own_ref, n1_ref, n2_ref, n3_ref = refs[exps + 3 :]
    height = z_ref.shape[0] - PR
    half = height // 2
    base = half * exps
    sub16 = iota((PR, PC), 0)
    hots = []
    for ref, at, first, invalid in (
        (z_ref, height, (0, 3), True), (m1_ref, base, (0, 2), False), (m2_ref, base, (0, 2), False),
    ):
        meta = ref[at : at + PR]
        for c in range(2):
            scale = jnp.where(sub16 == first[c], 32.0, jnp.where(sub16 == first[c] + 1, 1.0, 0.0))
            if invalid:
                scale = jnp.where(sub16 == 3 * c + 2, -2.0 * TR, scale)
            pos = dot(meta, scale.astype(BF16), 0, 0)[:half].astype(jnp.int32)
            lanes = iota((half, PC), 1)
            hots.append(
                jnp.concatenate(
                    [
                        jnp.where(lanes + PC * i == pos, 1.0, 0.0).astype(BF16)
                        for i in range(TR // PC)
                    ],
                    1,
                )
            )
    cut = dot(jnp.concatenate(hots, 0), template).astype(BF16)
    head = template[:PR]
    own_ref[...] = cut[:height]
    n1_ref[0:height] = cut[height : 2 * height]
    n1_ref[height : height + PR] = head
    n2_ref[0:height] = cut[2 * height :]
    n2_ref[height : height + PR] = head
    n3_ref[...] = head


def subtract_body(matched_ref, own_ref, n1_ref, n2_ref, n3_ref, z_ref, out_ref):
    height = own_ref.shape[0]
    half = height // 2
    lane = iota((height, PC), 1)
    sub16 = iota((PR, PC), 0)
    top = iota((height, PC), 0) < half
    meta = z_ref[height : height + PR]
    heads = [n1_ref[height : height + PR], n2_ref[height : height + PR], n3_ref[...]]
    heads.append(jnp.zeros((PC - REACH * PR, PC), BF16))
    heads = jnp.concatenate(heads, 0)
    for c in range(2):
        scale = jnp.where(sub16 == 3 * c, 32.0, jnp.where(sub16 == 3 * c + 1, 1.0, 0.0))
        over = dot(meta, scale.astype(BF16), 0, 0) - TR
        step = dot(meta, jnp.where(sub16 == 3 * c + 2, 1.0, 0.0).astype(BF16), 0, 0)
        at = jnp.where(over >= 0.0, over + PR * step, -1.0).astype(jnp.int32)
        own, mid, far = (r[half * c : half * (c + 1)].astype(F32) for r in (own_ref, n1_ref, n2_ref))
        inner = jnp.concatenate([mid, mid], 0)
        outer = jnp.concatenate([own, far], 0)
        back = jnp.where(step == jnp.where(top, 0.0, 2.0), outer, inner)
        back += dot(jnp.where(lane == at, 1.0, 0.0).astype(BF16), heads)
        out_ref[:, PC * c : PC * (c + 1)] = (matched_ref[:, PC * c : PC * (c + 1)] - back).astype(BF16)


VM = pl.BlockSpec(memory_space=pltpu.VMEM)
HBM = pl.BlockSpec(memory_space=pltpu.HBM)


def call(body, outs, specs, name, scratch=(), micros=1):
    return pl.pallas_call(
        body,
        out_shape=tuple(jax.ShapeDtypeStruct(s, t) for s, t in outs),
        in_specs=specs,
        out_specs=tuple(VM for _ in outs),
        scratch_shapes=scratch,
        compiler_params=PARAMS,
        cost_estimate=pl.CostEstimate(
            flops=micros * 10**9, bytes_accessed=micros * 10**6, transcendentals=0
        ),
        name=name,
    )


def along_exp(x, k, exps):
    return lax.ppermute(x, "exp", [(i, i ^ k) for i in range(exps)])


def along_tile(x, by, tiles):
    return lax.ppermute(x, "tile", [(i, (i + by) % tiles) for i in range(tiles)])


def program_of(exps, tiles):
    def body(science, mask_bits, variance, kernel_poly, basis_rows, basis_cols, destination, row_offset):
        height, across = science.shape[2:]
        half = height // 2
        message = ((height + PR, PC), BF16)
        args = (
            basis_rows, basis_cols, science.reshape(height, across),
            jnp.transpose(kernel_poly, (0, 3, 1, 2)), mask_bits.reshape(height, across),
            variance.reshape(height, across), destination.reshape(-1), row_offset.reshape(-1),
        )
        args = tuple(pltpu.with_memory_space_constraint(a, pltpu.HBM) for a in args)
        small = (3, 6, 7)
        matched, *z = call(
            lambda *r: match_body(exps, tiles, *r),
            [((height, across), F32)] + [message] * exps,
            [HBM] * len(args),
            "match",
            [(pltpu.SMEM if i in small else pltpu.VMEM)(a.shape, a.dtype) for i, a in enumerate(args)]
            + [pltpu.SemaphoreType.DMA((len(args),))],
        )(*args)
        z = [z[0]] + [along_exp(z[k], k, exps) for k in range(1, exps)]
        big = ((half * exps + PR * meta_tiles(exps) + 2 * PR, PC), BF16)
        m1, m2, m3 = call(
            lambda *r: pick_body(exps, *r), [big, big, ((2 * PR, PC), BF16)], [VM] * exps, "pick"
        )(*z)
        m1, m2, m3 = (along_tile(m, i + 1, tiles) for i, m in enumerate((m1, m2, m3)))
        (own,) = call(lambda *r: own_body(exps, *r), [((TR, PC), F32)], [VM] * exps, "own")(*z)
        (packed,) = call(
            lambda *r: sum_body(exps, *r), [((TR // exps, PC), BF16)], [VM] * 4, "sum"
        )(own, m1, m2, m3)
        packed = [packed] + [along_exp(packed, k, exps) for k in range(1, exps)]
        own, n1, n2, n3 = call(
            lambda *r: cut_body(exps, *r),
            [((height, PC), BF16), message, message, ((PR, PC), BF16)],
            [VM] * (exps + 3),
            "cut",
        )(*packed, z[0], m1, m2)
        n1, n2, n3 = (along_tile(n, -1 - i, tiles) for i, n in enumerate((n1, n2, n3)))
        (template,) = call(
            lambda *r: template_body(exps, *r), [((TR, PC), BF16)], [VM] * exps, "template"
        )(*packed)
        (difference,) = call(
            subtract_body, [((height, across), BF16)], [VM] * 6, "subtract"
        )(matched, own, n1, n2, n3, z[0])
        return template, difference[None, None]

    return body


def solution(mesh):
    placed = (
        P("exp", "tile", None, None),
        P("exp", "tile", None, None),
        P("exp", "tile", None, None),
        P("exp", "tile", None, None),
        P(),
        P(),
        P("exp", "tile", None, None),
        P("exp", "tile", None),
    )
    return jax.shard_map(
        program_of(mesh.shape["exp"], mesh.shape["tile"]),
        mesh=mesh,
        in_specs=placed,
        out_specs=(P("tile", None), P("exp", "tile", None, None)),
        check_vma=False,
    )
```

```python
import jax
import jax.numpy as jnp
from jax import lax
from jax.experimental import pallas as pl
from jax.experimental.pallas import tpu as pltpu
from jax.sharding import PartitionSpec as P


PR = 16
PC = 128
TR = 1024
F32 = jnp.float32
BF16 = jnp.bfloat16
SENT = 32.0
REACH = 3
PARAMS = pltpu.CompilerParams(vmem_limit_bytes=24 * 1024 * 1024)


def iota(shape, dim):
    return lax.broadcasted_iota(jnp.int32, shape, dim)


def dot(a, b, ca=1, cb=0):
    return lax.dot_general(a, b, (((ca,), (cb,)), ((), ())), preferred_element_type=F32)


def circulant(taps, reverse):
    count, ks = taps.shape
    half = ks // 2
    tap, lane = iota((ks, PC), 0), iota((ks, PC), 1)
    place = (half - tap) if reverse else (tap - half)
    pick = jnp.where((place + PC) % PC == lane, 1.0, 0.0).astype(BF16)
    row = dot(taps, pick)
    return [
        pltpu.roll(jnp.broadcast_to(row[b : b + 1], (PC, PC)), 0, 1, stride=1, stride_axis=0)
        for b in range(count)
    ]


def same_row(places, first, count):
    row = iota((count, PC), 0).astype(BF16)
    one, zero = jnp.ones((count, PC), BF16), jnp.zeros((count, PC), BF16)
    return jnp.concatenate(
        [jnp.where(row == (p - float(first)).astype(BF16), one, zero) for p in places], 1
    )


def meta_rows(meta, half):
    hi, lo, step = (meta[3 * half + i : 3 * half + i + 1] for i in range(3))
    return hi, lo, step


def spill_at(hi, lo, step):
    over = hi * 32.0 + lo - TR
    return jnp.where(over >= 0.0, over + PR * step, -1.0)


def meta_tiles(exps):
    return -(-2 * exps // PR)


def piece_scalars(dest_ref, off_ref, p, tile, tiles):
    target = dest_ref[p]
    offset = off_ref[p]
    offset = jnp.where(target == tiles - 1, jnp.minimum(offset, TR - PR), offset)
    return (target - tile + tiles) % tiles, offset


def match_body(exps, tiles, *refs):
    args, matched_ref, z_refs = refs[:8], refs[8], refs[9 : 9 + exps]
    held, sems = refs[9 + exps : 17 + exps], refs[17 + exps]
    copies = [pltpu.make_async_copy(a, h, sems.at[i]) for i, (a, h) in enumerate(zip(args, held))]
    for copy in copies:
        copy.start()
    brow_ref, bcol_ref, sci_ref, poly_ref, mask_ref, var_ref, dest_ref, off_ref = held
    exp, tile = lax.axis_index("exp"), lax.axis_index("tile")
    height, across = sci_ref.shape
    bases = brow_ref.shape[0]
    copies[0].wait()
    copies[1].wait()
    d = iota((PC, PC), 1) - iota((PC, PC), 0)
    zero = jnp.zeros((PC, PC), F32)
    cols = circulant(bcol_ref[...], True)
    rows = circulant(brow_ref[...], False)
    copies[2].wait()
    copies[3].wait()
    sci = sci_ref[...]
    y = (iota((height, across), 0).astype(F32) - (height - 1) / 2.0) / (height / 2.0)
    x = (iota((height, across), 1).astype(F32) - (across - 1) / 2.0) / (across / 2.0)
    matched = jnp.zeros((height, across), F32)
    for b in range(bases):
        mid = jnp.where(jnp.abs(d) < PC // 2, cols[b], zero)
        up = jnp.where(d < -(PC // 2), cols[b], zero)
        low = jnp.where(d > PC // 2, cols[b], zero)
        band = jnp.concatenate(
            [jnp.concatenate([mid, up], 1), jnp.concatenate([low, mid], 1)], 0
        ).astype(BF16)
        first = dot(sci, band).astype(BF16)
        row_band = jnp.where(jnp.abs(d) < PC // 2, rows[b], zero).astype(BF16)
        second = dot(row_band, first)
        matched += (poly_ref[0, 0, 0, b] + poly_ref[0, 1, 0, b] * y + poly_ref[0, 2, 0, b] * x) * second
    matched_ref[...] = matched
    for copy in copies[4:]:
        copy.wait()
    rejected = jnp.bitwise_and(mask_ref[...], 7) != 0
    weight = jnp.where(rejected, 0.0, 1.0 / var_ref[...].astype(F32))
    weighted = matched * weight
    half = height // 2
    share = PC // exps
    parts = refs[18 + exps]
    for h in range(2):
        for i, image in enumerate((weighted, weight)):
            rows_of = image[half * h : half * (h + 1)]
            stacked = jnp.concatenate([rows_of[:, :PC], rows_of[:, PC:]], 0)
            parts[2 * h + i] = stacked.T.astype(parts.dtype)
    lane = iota((1, PC), 1)
    sub = iota((PR, PC), 0)
    meta = jnp.zeros((PR, PC), F32)
    per_half = half // PR
    for h in range(2):
        pos = jnp.zeros((1, PC), jnp.int32)
        step = jnp.zeros((1, PC), jnp.int32)
        for c in range(2):
            for rb in range(per_half):
                piece = 2 * (per_half * h + rb) + c
                rel, offset = piece_scalars(dest_ref, off_ref, piece, tile, tiles)
                here = lane // PR == per_half * c + rb
                pos = jnp.where(here, offset + lane % PR, pos)
                step = jnp.where(here, rel, step)
        for i, v in enumerate((pos // 32, pos % 32, step)):
            meta = jnp.where(sub == 3 * h + i, v.astype(F32), meta)
    meta = meta.astype(BF16)
    for k in range(exps):
        at = pl.multiple_of(share * jnp.bitwise_xor(exp, k), share)
        for g in range(4):
            z_refs[k][share * g : share * (g + 1)] = parts[g, pl.ds(at, share)].astype(BF16)
        z_refs[k][4 * share : 4 * share + PR] = meta


def pick_body(exps, *refs):
    z_refs, (m1_ref, m2_ref, m3_ref) = refs[:exps], refs[exps:]
    share = PC // exps
    pair = 2 * share
    sub16 = iota((PR, PC), 0)
    spill_row = iota((REACH * PR, PC), 0).astype(F32)
    spill = jnp.zeros((REACH * PR, PC), F32)
    metas = [[jnp.zeros((PR, PC), F32) for _ in range(meta_tiles(exps))] for _ in range(2)]
    for k in range(exps):
        top, bottom = z_refs[k][0:pair], z_refs[k][pair : 2 * pair]
        meta = z_refs[k][2 * pair : 2 * pair + PR].astype(F32)
        (hi0, lo0, step0), (hi1, lo1, step1) = meta_rows(meta, 0), meta_rows(meta, 1)
        use_top = step0 == 1.0
        mixed = jnp.where(use_top, top.astype(F32), bottom.astype(F32)).astype(BF16)
        m1_ref[pair * k : pair * (k + 1)] = mixed
        m2_ref[pair * k : pair * (k + 1)] = bottom
        for data, at in ((top, spill_at(hi0, lo0, step0)), (bottom, spill_at(hi1, lo1, step1))):
            hot = jnp.where(spill_row == at, 1.0, 0.0).astype(BF16)
            spill += dot(hot, jnp.concatenate([data] * (PC // pair), 0), 1, 1)
        values = (
            (jnp.where(use_top, hi0, jnp.where(step1 == 1.0, hi1, -SENT)), jnp.where(use_top, lo0, lo1)),
            (jnp.where(step1 == 2.0, hi1, -SENT), lo1),
        )
        at, row = 2 * k // PR, 2 * k % PR
        for tiles_of, rows_of in zip(metas, values):
            for i, v in enumerate(rows_of):
                tiles_of[at] = jnp.where(sub16 == row + i, v, tiles_of[at])
    coarse = spill.astype(BF16)
    fine = (spill - coarse.astype(F32)).astype(BF16)
    both = jnp.where(
        iota((REACH * PR, PC), 1) < pair, coarse.astype(F32), fine.astype(F32)
    ).astype(BF16)
    base = pair * exps
    for s, (ref, tiles_of) in enumerate(((m1_ref, metas[0]), (m2_ref, metas[1]))):
        for i, m in enumerate(tiles_of):
            ref[base + PR * i : base + PR * (i + 1)] = m.astype(BF16)
        at = base + PR * len(tiles_of)
        ref[at : at + PR] = both[PR * s : PR * (s + 1)]
    m3_ref[...] = both[2 * PR :]


BLOCK = 256


def own_body(exps, *refs):
    z_refs, out_ref = refs[:exps], refs[exps]
    share = PC // exps
    pair = 2 * share
    data = jnp.concatenate([z[0:pair] for z in z_refs], 1)
    places = []
    for z in z_refs:
        hi, lo, step = meta_rows(z[2 * pair : 2 * pair + PR].astype(F32), 0)
        places.append(jnp.where(step == 0.0, hi * 32.0 + lo, -1.0))
    for q in range(TR // BLOCK):
        hot = same_row(places, BLOCK * q, BLOCK)
        out_ref[:, BLOCK * q : BLOCK * (q + 1)] = dot(data, hot, 1, 1)


def message_places(ref, exps, k):
    base = 2 * PC // exps * exps
    at, row = base + PR * (2 * k // PR), 2 * k % PR
    meta = ref[at : at + PR].astype(F32)
    return meta[row : row + 1] * 32.0 + meta[row + 1 : row + 2]


def sum_body(exps, own_ref, m1_ref, m2_ref, m3_ref, out_ref):
    share = PC // exps
    pair = 2 * share
    at = pair * exps + PR * meta_tiles(exps)
    refs = (m1_ref, m2_ref)
    data = jnp.concatenate([r[pair * k : pair * (k + 1)] for r in refs for k in range(exps)], 1)
    places = [message_places(r, exps, k) for r in refs for k in range(exps)]
    spill = m3_ref[...].astype(F32)
    for r in refs:
        spill += r[at : at + PR].astype(F32)
    spill += pltpu.roll(spill, PC - pair, 1)
    spill = jnp.concatenate([spill, jnp.zeros((PC - PR, PC), F32)], 0).T[:pair]
    for q in range(TR // BLOCK):
        lanes = slice(BLOCK * q, BLOCK * (q + 1))
        total = dot(data, same_row(places, BLOCK * q, BLOCK), 1, 1) + own_ref[:, lanes]
        if q == 0:
            total = jnp.concatenate([total[:, :PC] + spill, total[:, PC:]], 1)
        out_ref[:, lanes] = (total[:share] / jnp.maximum(total[share:], 1.0)).astype(BF16)


def cut_body(exps, *refs):
    packed_refs, (z_ref, m1_ref, m2_ref) = refs[:exps], refs[exps : exps + 3]
    tile_ref, own_ref, n1_ref, n2_ref, n3_ref = refs[exps + 3 :]
    exp = lax.axis_index("exp")
    share = PC // exps
    for k in range(exps):
        at = pl.multiple_of(share * jnp.bitwise_xor(exp, k), share)
        tile_ref[pl.ds(at, share)] = packed_refs[k][...].astype(tile_ref.dtype)
    tile = tile_ref[...].astype(BF16)
    hi, lo, step = meta_rows(z_ref[4 * share : 4 * share + PR].astype(F32), 0)
    places = [
        jnp.where(step == 0.0, hi * 32.0 + lo, -1.0),
        message_places(m1_ref, exps, 0),
        message_places(m2_ref, exps, 0),
    ]
    hot = jnp.concatenate([same_row(places, BLOCK * q, BLOCK) for q in range(TR // BLOCK)], 0)
    cut = dot(tile, hot).astype(BF16)
    head = tile[:, :PC].astype(F32).T[:PR].astype(BF16)
    own_ref[...] = cut[:, :PC]
    n1_ref[0:PC] = cut[:, PC : 2 * PC]
    n1_ref[PC : PC + PR] = head
    n2_ref[0:PC] = cut[:, 2 * PC :]
    n2_ref[PC : PC + PR] = head
    n3_ref[...] = head


def template_body(tile_ref, out_ref):
    for i in range(TR // PC):
        lanes = slice(PC * i, PC * (i + 1))
        out_ref[lanes] = tile_ref[:, lanes].astype(F32).T.astype(BF16)


def subtract_body(exps, matched_ref, own_ref, n1_ref, n2_ref, n3_ref, z_ref, out_ref):
    half = matched_ref.shape[0] // 2
    at = 4 * (PC // exps)
    meta = z_ref[at : at + PR].astype(F32)
    heads = [n1_ref[PC : PC + PR], n2_ref[PC : PC + PR], n3_ref[...]]
    heads.append(jnp.zeros((PC - REACH * PR, PC), BF16))
    heads = jnp.concatenate(heads, 0)
    row = iota((PC, PC), 0).astype(F32)
    middle = n1_ref[0:PC].astype(F32)
    for h, (ref, outer) in enumerate(((own_ref, 0.0), (n2_ref, 2.0))):
        hi, lo, step = meta_rows(meta, h)
        hot = jnp.where(row == spill_at(hi, lo, step), 1.0, 0.0).astype(BF16)
        back = jnp.where(step == outer, ref[0:PC].astype(F32), middle) + dot(heads, hot, 0, 0)
        back = back.T
        rows = slice(half * h, half * (h + 1))
        for c in range(2):
            lanes = slice(PC * c, PC * (c + 1))
            out_ref[rows, lanes] = (matched_ref[rows, lanes] - back[half * c : half * (c + 1)]).astype(BF16)


VM = pl.BlockSpec(memory_space=pltpu.VMEM)
HBM = pl.BlockSpec(memory_space=pltpu.HBM)


def call(body, outs, specs, scratch=(), micros=1):
    return pl.pallas_call(
        body,
        out_shape=tuple(jax.ShapeDtypeStruct(s, t) for s, t in outs),
        in_specs=specs,
        out_specs=tuple(VM for _ in outs),
        scratch_shapes=scratch,
        compiler_params=PARAMS,
        cost_estimate=pl.CostEstimate(
            flops=micros * 10**9, bytes_accessed=micros * 10**6, transcendentals=0
        ),
    )


def along_exp(x, k, exps):
    return lax.ppermute(x, "exp", [(i, i ^ k) for i in range(exps)])


def along_tile(x, by, tiles):
    return lax.ppermute(x, "tile", [(i, (i + by) % tiles) for i in range(tiles)])


def program_of(exps, tiles):
    def steps(science, mask_bits, variance, kernel_poly, basis_rows, basis_cols, destination, row_offset):
        height, across = science.shape[2:]
        share = PC // exps
        packs = BF16 if share % 16 == 0 else F32
        message = ((4 * share + PR, PC), BF16)
        args = (
            basis_rows, basis_cols, science.reshape(height, across),
            jnp.transpose(kernel_poly, (0, 3, 1, 2)), mask_bits.reshape(height, across),
            variance.reshape(height, across), destination.reshape(-1), row_offset.reshape(-1),
        )
        args = tuple(pltpu.with_memory_space_constraint(a, pltpu.HBM) for a in args)
        small = (3, 6, 7)
        matched, *z = call(
            lambda *r: match_body(exps, tiles, *r),
            [((height, across), F32)] + [message] * exps,
            [HBM] * len(args),
            [(pltpu.SMEM if i in small else pltpu.VMEM)(a.shape, a.dtype) for i, a in enumerate(args)]
            + [pltpu.SemaphoreType.DMA((len(args),)), pltpu.VMEM((4, PC, PC), packs)],
        )(*args)
        z = [z[0]] + [along_exp(z[k], k, exps) for k in range(1, exps)]
        big = ((2 * share * exps + PR * meta_tiles(exps) + PR, PC), BF16)
        m1, m2, m3 = call(lambda *r: pick_body(exps, *r), [big, big, ((PR, PC), BF16)], [VM] * exps)(*z)
        m1, m2, m3 = (along_tile(m, i + 1, tiles) for i, m in enumerate((m1, m2, m3)))
        (own,) = call(lambda *r: own_body(exps, *r), [((2 * share, TR), F32)], [VM] * exps)(*z)
        (packed,) = call(lambda *r: sum_body(exps, *r), [((share, TR), BF16)], [VM] * 4)(own, m1, m2, m3)
        packed = [packed] + [along_exp(packed, k, exps) for k in range(1, exps)]
        back = ((PC + PR, PC), BF16)
        tile, own, n1, n2, n3 = call(
            lambda *r: cut_body(exps, *r),
            [((PC, TR), packs), ((PC, PC), BF16), back, back, ((PR, PC), BF16)],
            [VM] * (exps + 3),
        )(*packed, z[0], m1, m2)
        n1, n2, n3 = (along_tile(n, -1 - i, tiles) for i, n in enumerate((n1, n2, n3)))
        (template,) = call(template_body, [((TR, PC), BF16)], [VM])(tile)
        (difference,) = call(
            lambda *r: subtract_body(exps, *r), [((height, across), BF16)], [VM] * 6
        )(matched, own, n1, n2, n3, z[0])
        return template, difference[None, None]

    return steps


def solution(mesh):
    placed = (
        P("exp", "tile", None, None),
        P("exp", "tile", None, None),
        P("exp", "tile", None, None),
        P("exp", "tile", None, None),
        P(),
        P(),
        P("exp", "tile", None, None),
        P("exp", "tile", None),
    )
    return jax.shard_map(
        program_of(mesh.shape["exp"], mesh.shape["tile"]),
        mesh=mesh,
        in_specs=placed,
        out_specs=(P("tile", None), P("exp", "tile", None, None)),
        check_vma=False,
    )
```

```python
import jax
import jax.numpy as jnp
from jax import lax
from jax.experimental import pallas as pl
from jax.experimental.pallas import tpu as pltpu
from jax.sharding import PartitionSpec as P


PR = 16
PC = 128
TR = 1024
F32 = jnp.float32
BF16 = jnp.bfloat16
SENT = 32.0
REACH = 3
PARAMS = pltpu.CompilerParams(vmem_limit_bytes=24 * 1024 * 1024)


def iota(shape, dim):
    return lax.broadcasted_iota(jnp.int32, shape, dim)


def dot(a, b, ca=1, cb=0):
    return lax.dot_general(a, b, (((ca,), (cb,)), ((), ())), preferred_element_type=F32)


def circulant(taps, reverse):
    count, ks = taps.shape
    half = ks // 2
    tap, lane = iota((ks, PC), 0), iota((ks, PC), 1)
    place = (half - tap) if reverse else (tap - half)
    pick = jnp.where((place + PC) % PC == lane, 1.0, 0.0).astype(BF16)
    row = dot(taps, pick)
    return [
        pltpu.roll(jnp.broadcast_to(row[b : b + 1], (PC, PC)), 0, 1, stride=1, stride_axis=0)
        for b in range(count)
    ]


def same_row(places, first, count):
    row = iota((count, PC), 0).astype(BF16)
    one, zero = jnp.ones((count, PC), BF16), jnp.zeros((count, PC), BF16)
    return jnp.concatenate(
        [jnp.where(row == (p - float(first)).astype(BF16), one, zero) for p in places], 1
    )


def meta_rows(meta, half):
    hi, lo, step = (meta[3 * half + i : 3 * half + i + 1] for i in range(3))
    return hi, lo, step


def spill_at(hi, lo, step):
    over = hi * 32.0 + lo - TR
    return jnp.where(over >= 0.0, over + PR * step, -1.0)


def meta_tiles(exps):
    return -(-2 * exps // PR)


def match_body(exps, tiles, *refs):
    args, matched_ref, z_refs = refs[:8], refs[8], refs[9 : 9 + exps]
    held, sems = refs[9 + exps : 17 + exps], refs[17 + exps]
    copies = [pltpu.make_async_copy(a, h, sems.at[i]) for i, (a, h) in enumerate(zip(args, held))]
    for copy in copies:
        copy.start()
    brow_ref, bcol_ref, sci_ref, poly_ref, mask_ref, var_ref, dest_ref, off_ref = held
    exp, tile = lax.axis_index("exp"), lax.axis_index("tile")
    height, across = sci_ref.shape
    bases = brow_ref.shape[0]
    copies[0].wait()
    copies[1].wait()
    d = iota((PC, PC), 1) - iota((PC, PC), 0)
    zero = jnp.zeros((PC, PC), F32)
    cols = circulant(bcol_ref[...], True)
    rows = circulant(brow_ref[...], False)
    for copy in copies[2:]:
        copy.wait()
    half = height // 2
    share = PC // exps
    pieces = dest_ref.shape[1]
    target, offset = dest_ref[...], off_ref[...]
    offset = jnp.where(target == tiles - 1, jnp.minimum(offset, TR - PR), offset)
    step = target - tile
    step = jnp.where(step < 0, step + tiles, step)
    known = jnp.concatenate(
        [(offset // 32).astype(F32), (offset % 32).astype(F32), step.astype(F32)]
        + [jnp.zeros((PR - 3, pieces), F32)],
        0,
    ).astype(BF16)
    piece, lane = iota((pieces, PC), 0), iota((pieces, PC), 1)
    per_half = half // PR
    sub = iota((PR, PC), 0)
    meta = jnp.zeros((PR, PC), F32)
    for h in range(2):
        under = 2 * (per_half * h + lane // PR % per_half) + lane // half
        spread = dot(known, jnp.where(piece == under, 1.0, 0.0).astype(BF16))
        pos = (spread[0:1] * 32.0 + spread[1:2]).astype(jnp.int32) + iota((1, PC), 1) % PR
        for i, v in enumerate(((pos // 32).astype(F32), (pos % 32).astype(F32), spread[2:3])):
            meta = jnp.where(sub == 3 * h + i, v, meta)
    meta = meta.astype(BF16)
    sci = sci_ref[...]
    y = (iota((height, 1), 0).astype(F32) - (height - 1) / 2.0) / (height / 2.0)
    x = (iota((1, across), 1).astype(F32) - (across - 1) / 2.0) / (across / 2.0)
    matched = jnp.zeros((height, across), F32)
    bands = []
    for b in range(bases):
        mid = jnp.where(jnp.abs(d) < PC // 2, cols[b], zero)
        up = jnp.where(d < -(PC // 2), cols[b], zero)
        low = jnp.where(d > PC // 2, cols[b], zero)
        bands.append(
            jnp.concatenate([jnp.concatenate([mid, up], 1), jnp.concatenate([low, mid], 1)], 0).astype(BF16)
        )
    first = dot(sci, jnp.concatenate(bands, 1)).astype(BF16)
    for b in range(bases):
        row_band = jnp.where(jnp.abs(d) < PC // 2, rows[b], zero).astype(BF16)
        second = dot(row_band, first[:, across * b : across * (b + 1)])
        along = jnp.broadcast_to(poly_ref[0, 0, 0, b] + poly_ref[0, 1, 0, b] * y, (height, across))
        matched += (along + poly_ref[0, 2, 0, b] * x) * second
    matched_ref[...] = matched
    rejected = jnp.bitwise_and(mask_ref[...], 7) != 0
    weight = jnp.where(rejected, 0.0, 1.0 / var_ref[...].astype(F32))
    weighted = matched * weight
    parts = refs[18 + exps]
    for h in range(2):
        for i, image in enumerate((weighted, weight)):
            rows_of = image[half * h : half * (h + 1)]
            stacked = jnp.concatenate([rows_of[:, :PC], rows_of[:, PC:]], 0)
            parts[2 * h + i] = stacked.T.astype(parts.dtype)
    for k in range(exps):
        at = pl.multiple_of(share * jnp.bitwise_xor(exp, k), share)
        for g in range(4):
            z_refs[k][share * g : share * (g + 1)] = parts[g, pl.ds(at, share)].astype(BF16)
        z_refs[k][4 * share : 4 * share + PR] = meta


def pick_body(exps, *refs):
    z_refs, (m1_ref, m2_ref, m3_ref) = refs[:exps], refs[exps:]
    share = PC // exps
    pair = 2 * share
    sub16 = iota((PR, PC), 0)
    spill_row = iota((REACH * PR, PC), 0).astype(F32)
    spill = jnp.zeros((REACH * PR, PC), F32)
    metas = [[jnp.zeros((PR, PC), F32) for _ in range(meta_tiles(exps))] for _ in range(2)]
    for k in range(exps):
        top, bottom = z_refs[k][0:pair], z_refs[k][pair : 2 * pair]
        meta = z_refs[k][2 * pair : 2 * pair + PR].astype(F32)
        (hi0, lo0, step0), (hi1, lo1, step1) = meta_rows(meta, 0), meta_rows(meta, 1)
        use_top = step0 == 1.0
        mixed = jnp.where(use_top, top.astype(F32), bottom.astype(F32)).astype(BF16)
        m1_ref[pair * k : pair * (k + 1)] = mixed
        m2_ref[pair * k : pair * (k + 1)] = bottom
        for data, at in ((top, spill_at(hi0, lo0, step0)), (bottom, spill_at(hi1, lo1, step1))):
            hot = jnp.where(spill_row == at, 1.0, 0.0).astype(BF16)
            spill += dot(hot, jnp.concatenate([data] * (PC // pair), 0), 1, 1)
        values = (
            (jnp.where(use_top, hi0, jnp.where(step1 == 1.0, hi1, -SENT)), jnp.where(use_top, lo0, lo1)),
            (jnp.where(step1 == 2.0, hi1, -SENT), lo1),
        )
        at, row = 2 * k // PR, 2 * k % PR
        for tiles_of, rows_of in zip(metas, values):
            for i, v in enumerate(rows_of):
                tiles_of[at] = jnp.where(sub16 == row + i, v, tiles_of[at])
    coarse = spill.astype(BF16)
    fine = (spill - coarse.astype(F32)).astype(BF16)
    both = jnp.where(
        iota((REACH * PR, PC), 1) < pair, coarse.astype(F32), fine.astype(F32)
    ).astype(BF16)
    base = pair * exps
    for s, (ref, tiles_of) in enumerate(((m1_ref, metas[0]), (m2_ref, metas[1]))):
        for i, m in enumerate(tiles_of):
            ref[base + PR * i : base + PR * (i + 1)] = m.astype(BF16)
        at = base + PR * len(tiles_of)
        ref[at : at + PR] = both[PR * s : PR * (s + 1)]
    m3_ref[...] = both[2 * PR :]


BLOCK = 256


def own_body(exps, *refs):
    z_refs, out_ref = refs[:exps], refs[exps]
    share = PC // exps
    pair = 2 * share
    data = jnp.concatenate([z[0:pair] for z in z_refs], 1)
    places = []
    for z in z_refs:
        hi, lo, step = meta_rows(z[2 * pair : 2 * pair + PR].astype(F32), 0)
        places.append(jnp.where(step == 0.0, hi * 32.0 + lo, -1.0))
    for q in range(TR // BLOCK):
        hot = same_row(places, BLOCK * q, BLOCK)
        out_ref[:, BLOCK * q : BLOCK * (q + 1)] = dot(data, hot, 1, 1)


def message_places(ref, exps, k):
    base = 2 * PC // exps * exps
    at, row = base + PR * (2 * k // PR), 2 * k % PR
    meta = ref[at : at + PR].astype(F32)
    return meta[row : row + 1] * 32.0 + meta[row + 1 : row + 2]


def message_sums(exps, prior_ref, ref, q):
    pair = 2 * PC // exps
    data = jnp.concatenate([ref[pair * k : pair * (k + 1)] for k in range(exps)], 1)
    places = [message_places(ref, exps, k) for k in range(exps)]
    lanes = slice(BLOCK * q, BLOCK * (q + 1))
    return dot(data, same_row(places, BLOCK * q, BLOCK), 1, 1) + prior_ref[:, lanes]


def far_body(exps, own_ref, m2_ref, out_ref):
    for q in range(TR // BLOCK):
        out_ref[:, BLOCK * q : BLOCK * (q + 1)] = message_sums(exps, own_ref, m2_ref, q)


def sum_body(exps, far_ref, m1_ref, m2_ref, m3_ref, out_ref):
    share = PC // exps
    pair = 2 * share
    at = pair * exps + PR * meta_tiles(exps)
    spill = m3_ref[...].astype(F32)
    for r in (m1_ref, m2_ref):
        spill += r[at : at + PR].astype(F32)
    spill += pltpu.roll(spill, PC - pair, 1)
    spill = jnp.concatenate([spill, jnp.zeros((PC - PR, PC), F32)], 0).T[:pair]
    for q in range(TR // BLOCK):
        total = message_sums(exps, far_ref, m1_ref, q)
        if q == 0:
            total = jnp.concatenate([total[:, :PC] + spill, total[:, PC:]], 1)
        lanes = slice(BLOCK * q, BLOCK * (q + 1))
        out_ref[:, lanes] = (total[:share] / jnp.maximum(total[share:], 1.0)).astype(BF16)


def place_body(exps, m1_ref, m2_ref, z_ref, hot_ref, own_ref):
    share = PC // exps
    hi, lo, step = meta_rows(z_ref[4 * share : 4 * share + PR].astype(F32), 0)
    own = [jnp.where(step == 0.0, hi * 32.0 + lo, -1.0)]
    others = [message_places(r, exps, 0) for r in (m1_ref, m2_ref)]
    for q in range(TR // BLOCK):
        rows = slice(BLOCK * q, BLOCK * (q + 1))
        hot_ref[rows] = same_row(others, BLOCK * q, BLOCK)
        own_ref[rows] = same_row(own, BLOCK * q, BLOCK)


def cut_body(exps, *refs):
    packed_refs, hot_ref, (tile_ref, n1_ref, n2_ref, n3_ref) = refs[:exps], refs[exps], refs[exps + 1 :]
    exp = lax.axis_index("exp")
    share = PC // exps
    for k in range(exps):
        at = pl.multiple_of(share * jnp.bitwise_xor(exp, k), share)
        tile_ref[pl.ds(at, share)] = packed_refs[k][...].astype(tile_ref.dtype)
    tile = tile_ref[...].astype(BF16)
    cut = dot(tile, hot_ref[...]).astype(BF16)
    head = tile[:, :PC].astype(F32).T[:PR].astype(BF16)
    n1_ref[0:PC] = cut[:, :PC]
    n1_ref[PC : PC + PR] = head
    n2_ref[0:PC] = cut[:, PC:]
    n2_ref[PC : PC + PR] = head
    n3_ref[...] = head


def template_body(tile_ref, hot_ref, out_ref, own_ref):
    for i in range(TR // PC):
        lanes = slice(PC * i, PC * (i + 1))
        out_ref[lanes] = tile_ref[:, lanes].astype(F32).T.astype(BF16)
    own_ref[...] = dot(tile_ref[...].astype(BF16), hot_ref[...]).astype(BF16)


def subtract_body(exps, matched_ref, own_ref, n1_ref, n2_ref, n3_ref, z_ref, out_ref):
    half = matched_ref.shape[0] // 2
    at = 4 * (PC // exps)
    meta = z_ref[at : at + PR].astype(F32)
    heads = [n1_ref[PC : PC + PR], n2_ref[PC : PC + PR], n3_ref[...]]
    heads.append(jnp.zeros((PC - REACH * PR, PC), BF16))
    heads = jnp.concatenate(heads, 0)
    row = iota((PC, PC), 0).astype(F32)
    middle = n1_ref[0:PC].astype(F32)
    for h, (ref, outer) in enumerate(((own_ref, 0.0), (n2_ref, 2.0))):
        hi, lo, step = meta_rows(meta, h)
        hot = jnp.where(row == spill_at(hi, lo, step), 1.0, 0.0).astype(BF16)
        back = jnp.where(step == outer, ref[0:PC].astype(F32), middle) + dot(heads, hot, 0, 0)
        back = back.T
        rows = slice(half * h, half * (h + 1))
        for c in range(2):
            lanes = slice(PC * c, PC * (c + 1))
            out_ref[rows, lanes] = (matched_ref[rows, lanes] - back[half * c : half * (c + 1)]).astype(BF16)


VM = pl.BlockSpec(memory_space=pltpu.VMEM)
HBM = pl.BlockSpec(memory_space=pltpu.HBM)


def call(body, outs, specs, scratch=(), micros=1):
    return pl.pallas_call(
        body,
        out_shape=tuple(jax.ShapeDtypeStruct(s, t) for s, t in outs),
        in_specs=specs,
        out_specs=tuple(VM for _ in outs),
        scratch_shapes=scratch,
        compiler_params=PARAMS,
        cost_estimate=pl.CostEstimate(
            flops=micros * 10**9, bytes_accessed=micros * 10**6, transcendentals=0
        ),
    )


def along_exp(x, k, exps):
    return lax.ppermute(x, "exp", [(i, i ^ k) for i in range(exps)])


def along_tile(x, by, tiles):
    return lax.ppermute(x, "tile", [(i, (i + by) % tiles) for i in range(tiles)])


def program_of(exps, tiles):
    def steps(science, mask_bits, variance, kernel_poly, basis_rows, basis_cols, destination, row_offset):
        height, across = science.shape[2:]
        share = PC // exps
        packs = BF16 if share % 16 == 0 else F32
        message = ((4 * share + PR, PC), BF16)
        args = (
            basis_rows, basis_cols, science.reshape(height, across),
            jnp.transpose(kernel_poly, (0, 3, 1, 2)), mask_bits.reshape(height, across),
            variance.reshape(height, across), destination.reshape(1, -1), row_offset.reshape(1, -1),
        )
        args = tuple(pltpu.with_memory_space_constraint(a, pltpu.HBM) for a in args)
        matched, *z = call(
            lambda *r: match_body(exps, tiles, *r),
            [((height, across), F32)] + [message] * exps,
            [HBM] * len(args),
            [(pltpu.SMEM if i == 3 else pltpu.VMEM)(a.shape, a.dtype) for i, a in enumerate(args)]
            + [pltpu.SemaphoreType.DMA((len(args),)), pltpu.VMEM((4, PC, PC), packs)],
        )(*args)
        z = [z[0]] + [along_exp(z[k], k, exps) for k in range(1, exps)]
        big = ((2 * share * exps + PR * meta_tiles(exps) + PR, PC), BF16)
        m1, m2, m3 = call(lambda *r: pick_body(exps, *r), [big, big, ((PR, PC), BF16)], [VM] * exps)(*z)
        m1, m2, m3 = (along_tile(m, i + 1, tiles) for i, m in enumerate((m1, m2, m3)))
        (own,) = call(lambda *r: own_body(exps, *r), [((2 * share, TR), F32)], [VM] * exps)(*z)
        (far,) = call(lambda *r: far_body(exps, *r), [((2 * share, TR), F32)], [VM] * 2)(own, m2)
        (packed,) = call(lambda *r: sum_body(exps, *r), [((share, TR), BF16)], [VM] * 4)(far, m1, m2, m3)
        packed = [packed] + [along_exp(packed, k, exps) for k in range(1, exps)]
        hot, own_hot = call(
            lambda *r: place_body(exps, *r), [((TR, 2 * PC), BF16), ((TR, PC), BF16)], [VM] * 3
        )(m1, m2, z[0])
        back = ((PC + PR, PC), BF16)
        tile, n1, n2, n3 = call(
            lambda *r: cut_body(exps, *r), [((PC, TR), packs), back, back, ((PR, PC), BF16)], [VM] * (exps + 1)
        )(*packed, hot)
        n1, n2, n3 = (along_tile(n, -1 - i, tiles) for i, n in enumerate((n1, n2, n3)))
        template, own = call(template_body, [((TR, PC), BF16), ((PC, PC), BF16)], [VM] * 2)(tile, own_hot)
        (difference,) = call(
            lambda *r: subtract_body(exps, *r), [((height, across), BF16)], [VM] * 6
        )(matched, own, n1, n2, n3, z[0])
        return template, difference[None, None]

    return steps


def solution(mesh):
    placed = (
        P("exp", "tile", None, None),
        P("exp", "tile", None, None),
        P("exp", "tile", None, None),
        P("exp", "tile", None, None),
        P(),
        P(),
        P("exp", "tile", None, None),
        P("exp", "tile", None),
    )
    return jax.shard_map(
        program_of(mesh.shape["exp"], mesh.shape["tile"]),
        mesh=mesh,
        in_specs=placed,
        out_specs=(P("tile", None), P("exp", "tile", None, None)),
        check_vma=False,
    )
```

```python
import jax
import jax.numpy as jnp
from jax import lax
from jax.experimental import pallas as pl
from jax.experimental.pallas import tpu as pltpu
from jax.sharding import PartitionSpec as P


PR = 16
PC = 128
TR = 1024
F32 = jnp.float32
BF16 = jnp.bfloat16
SENT = 32.0
REACH = 3
PARAMS = pltpu.CompilerParams(vmem_limit_bytes=24 * 1024 * 1024)


def iota(shape, dim):
    return lax.broadcasted_iota(jnp.int32, shape, dim)


def dot(a, b, ca=1, cb=0):
    return lax.dot_general(a, b, (((ca,), (cb,)), ((), ())), preferred_element_type=F32)


def partners(exps, name):
    far = list(range(4, exps))
    near = {"share": ((2, 3, 1), (2, 3, 1)), "join": ((3, 1, 2), (2, 3, 1))}[name]
    return [[0, *order[:2], *far, order[2]] for order in near]


def met_group(exps, name, i):
    exp, odd = lax.axis_index("exp"), lax.axis_index("tile") % 2
    even_way, odd_way = (order[i] for order in partners(exps, name))
    return jnp.bitwise_xor(exp, jnp.where(odd == 1, odd_way, even_way))


def circulant(taps, reverse):
    count, ks = taps.shape
    half = ks // 2
    tap, lane = iota((ks, PC), 0), iota((ks, PC), 1)
    place = (half - tap) if reverse else (tap - half)
    pick = jnp.where((place + PC) % PC == lane, 1.0, 0.0).astype(BF16)
    row = dot(taps, pick)
    return [
        pltpu.roll(jnp.broadcast_to(row[b : b + 1], (PC, PC)), 0, 1, stride=1, stride_axis=0)
        for b in range(count)
    ]


def same_row(places, first, count):
    row = iota((count, PC), 0).astype(BF16)
    one, zero = jnp.ones((count, PC), BF16), jnp.zeros((count, PC), BF16)
    return jnp.concatenate(
        [jnp.where(row == (p - float(first)).astype(BF16), one, zero) for p in places], 1
    )


def meta_rows(meta, half):
    hi, lo, step = (meta[3 * half + i : 3 * half + i + 1] for i in range(3))
    return hi, lo, step


def spill_at(hi, lo, step):
    over = hi * 32.0 + lo - TR
    return jnp.where(over >= 0.0, over + PR * step, -1.0)


def meta_tiles(exps):
    return -(-2 * exps // PR)


def match_body(exps, tiles, *refs):
    args, matched_ref, z_refs = refs[:8], refs[8], refs[9 : 9 + exps]
    held, sems = refs[9 + exps : 17 + exps], refs[17 + exps]
    copies = [pltpu.make_async_copy(a, h, sems.at[i]) for i, (a, h) in enumerate(zip(args, held))]
    for copy in copies:
        copy.start()
    brow_ref, bcol_ref, sci_ref, poly_ref, mask_ref, var_ref, dest_ref, off_ref = held
    tile = lax.axis_index("tile")
    height, across = sci_ref.shape
    bases = brow_ref.shape[0]
    copies[0].wait()
    copies[1].wait()
    d = iota((PC, PC), 1) - iota((PC, PC), 0)
    zero = jnp.zeros((PC, PC), F32)
    cols = circulant(bcol_ref[...], True)
    rows = circulant(brow_ref[...], False)
    for copy in copies[2:]:
        copy.wait()
    half = height // 2
    share = PC // exps
    pieces = dest_ref.shape[1]
    target, offset = dest_ref[...], off_ref[...]
    offset = jnp.where(target == tiles - 1, jnp.minimum(offset, TR - PR), offset)
    step = target - tile
    step = jnp.where(step < 0, step + tiles, step)
    known = jnp.concatenate(
        [(offset // 32).astype(F32), (offset % 32).astype(F32), step.astype(F32)]
        + [jnp.zeros((PR - 3, pieces), F32)],
        0,
    ).astype(BF16)
    piece, lane = iota((pieces, PC), 0), iota((pieces, PC), 1)
    per_half = half // PR
    sub = iota((PR, PC), 0)
    meta = jnp.zeros((PR, PC), F32)
    for h in range(2):
        under = 2 * (per_half * h + lane // PR % per_half) + lane // half
        spread = dot(known, jnp.where(piece == under, 1.0, 0.0).astype(BF16))
        pos = (spread[0:1] * 32.0 + spread[1:2]).astype(jnp.int32) + iota((1, PC), 1) % PR
        for i, v in enumerate(((pos // 32).astype(F32), (pos % 32).astype(F32), spread[2:3])):
            meta = jnp.where(sub == 3 * h + i, v, meta)
    meta = meta.astype(BF16)
    sci = sci_ref[...]
    y = (iota((height, 1), 0).astype(F32) - (height - 1) / 2.0) / (height / 2.0)
    x = (iota((1, across), 1).astype(F32) - (across - 1) / 2.0) / (across / 2.0)
    matched = jnp.zeros((height, across), F32)
    bands = []
    for b in range(bases):
        mid = jnp.where(jnp.abs(d) < PC // 2, cols[b], zero)
        up = jnp.where(d < -(PC // 2), cols[b], zero)
        low = jnp.where(d > PC // 2, cols[b], zero)
        bands.append(
            jnp.concatenate([jnp.concatenate([mid, up], 1), jnp.concatenate([low, mid], 1)], 0).astype(BF16)
        )
    first = dot(sci, jnp.concatenate(bands, 1)).astype(BF16)
    for b in range(bases):
        row_band = jnp.where(jnp.abs(d) < PC // 2, rows[b], zero).astype(BF16)
        second = dot(row_band, first[:, across * b : across * (b + 1)])
        along = jnp.broadcast_to(poly_ref[0, 0, 0, b] + poly_ref[0, 1, 0, b] * y, (height, across))
        matched += (along + poly_ref[0, 2, 0, b] * x) * second
    matched_ref[...] = matched
    rejected = jnp.bitwise_and(mask_ref[...], 7) != 0
    weight = jnp.where(rejected, 0.0, 1.0 / var_ref[...].astype(F32))
    weighted = matched * weight
    parts = refs[18 + exps]
    for h in range(2):
        for i, image in enumerate((weighted, weight)):
            rows_of = image[half * h : half * (h + 1)]
            stacked = jnp.concatenate([rows_of[:, :PC], rows_of[:, PC:]], 0)
            parts[2 * h + i] = stacked.T.astype(parts.dtype)
    for k in range(exps):
        at = pl.multiple_of(share * met_group(exps, "share", k), share)
        for g in range(4):
            z_refs[k][share * g : share * (g + 1)] = parts[g, pl.ds(at, share)].astype(BF16)
        z_refs[k][4 * share : 4 * share + PR] = meta


def pick_body(exps, *refs):
    z_refs, (m1_ref, m2_ref, m3_ref) = refs[:exps], refs[exps:]
    share = PC // exps
    pair = 2 * share
    sub16 = iota((PR, PC), 0)
    spill_row = iota((REACH * PR, PC), 0).astype(F32)
    spill = jnp.zeros((REACH * PR, PC), F32)
    metas = [[jnp.zeros((PR, PC), F32) for _ in range(meta_tiles(exps))] for _ in range(2)]
    for k in range(exps):
        top, bottom = z_refs[k][0:pair], z_refs[k][pair : 2 * pair]
        meta = z_refs[k][2 * pair : 2 * pair + PR].astype(F32)
        (hi0, lo0, step0), (hi1, lo1, step1) = meta_rows(meta, 0), meta_rows(meta, 1)
        use_top = step0 == 1.0
        mixed = jnp.where(use_top, top.astype(F32), bottom.astype(F32)).astype(BF16)
        m1_ref[pair * k : pair * (k + 1)] = mixed
        m2_ref[pair * k : pair * (k + 1)] = bottom
        for data, at in ((top, spill_at(hi0, lo0, step0)), (bottom, spill_at(hi1, lo1, step1))):
            hot = jnp.where(spill_row == at, 1.0, 0.0).astype(BF16)
            spill += dot(hot, jnp.concatenate([data] * (PC // pair), 0), 1, 1)
        values = (
            (jnp.where(use_top, hi0, jnp.where(step1 == 1.0, hi1, -SENT)), jnp.where(use_top, lo0, lo1)),
            (jnp.where(step1 == 2.0, hi1, -SENT), lo1),
        )
        at, row = 2 * k // PR, 2 * k % PR
        for tiles_of, rows_of in zip(metas, values):
            for i, v in enumerate(rows_of):
                tiles_of[at] = jnp.where(sub16 == row + i, v, tiles_of[at])
    coarse = spill.astype(BF16)
    fine = (spill - coarse.astype(F32)).astype(BF16)
    both = jnp.where(
        iota((REACH * PR, PC), 1) < pair, coarse.astype(F32), fine.astype(F32)
    ).astype(BF16)
    base = pair * exps
    for s, (ref, tiles_of) in enumerate(((m1_ref, metas[0]), (m2_ref, metas[1]))):
        for i, m in enumerate(tiles_of):
            ref[base + PR * i : base + PR * (i + 1)] = m.astype(BF16)
        at = base + PR * len(tiles_of)
        ref[at : at + PR] = both[PR * s : PR * (s + 1)]
    m3_ref[...] = both[2 * PR :]


BLOCK = 256


def own_body(exps, *refs):
    z_refs, out_ref = refs[:exps], refs[exps]
    share = PC // exps
    pair = 2 * share
    data = jnp.concatenate([z[0:pair] for z in z_refs], 1)
    places = []
    for z in z_refs:
        hi, lo, step = meta_rows(z[2 * pair : 2 * pair + PR].astype(F32), 0)
        places.append(jnp.where(step == 0.0, hi * 32.0 + lo, -1.0))
    for q in range(TR // BLOCK):
        hot = same_row(places, BLOCK * q, BLOCK)
        out_ref[:, BLOCK * q : BLOCK * (q + 1)] = dot(data, hot, 1, 1)


def message_places(ref, exps, k):
    base = 2 * PC // exps * exps
    at, row = base + PR * (2 * k // PR), 2 * k % PR
    meta = ref[at : at + PR].astype(F32)
    return meta[row : row + 1] * 32.0 + meta[row + 1 : row + 2]


def message_sums(exps, prior_ref, ref, q):
    pair = 2 * PC // exps
    data = jnp.concatenate([ref[pair * k : pair * (k + 1)] for k in range(exps)], 1)
    places = [message_places(ref, exps, k) for k in range(exps)]
    lanes = slice(BLOCK * q, BLOCK * (q + 1))
    return dot(data, same_row(places, BLOCK * q, BLOCK), 1, 1) + prior_ref[:, lanes]


def far_body(exps, own_ref, m2_ref, out_ref):
    for q in range(TR // BLOCK):
        out_ref[:, BLOCK * q : BLOCK * (q + 1)] = message_sums(exps, own_ref, m2_ref, q)


def sum_body(exps, far_ref, m1_ref, m2_ref, m3_ref, out_ref):
    share = PC // exps
    pair = 2 * share
    at = pair * exps + PR * meta_tiles(exps)
    spill = m3_ref[...].astype(F32)
    for r in (m1_ref, m2_ref):
        spill += r[at : at + PR].astype(F32)
    spill += pltpu.roll(spill, PC - pair, 1)
    spill = jnp.concatenate([spill, jnp.zeros((PC - PR, PC), F32)], 0).T[:pair]
    for q in range(TR // BLOCK):
        total = message_sums(exps, far_ref, m1_ref, q)
        if q == 0:
            total = jnp.concatenate([total[:, :PC] + spill, total[:, PC:]], 1)
        lanes = slice(BLOCK * q, BLOCK * (q + 1))
        out_ref[:, lanes] = (total[:share] / jnp.maximum(total[share:], 1.0)).astype(BF16)


def place_body(exps, m1_ref, m2_ref, z_ref, hot_ref, own_ref):
    share = PC // exps
    hi, lo, step = meta_rows(z_ref[4 * share : 4 * share + PR].astype(F32), 0)
    own = [jnp.where(step == 0.0, hi * 32.0 + lo, -1.0)]
    others = [message_places(r, exps, 0) for r in (m1_ref, m2_ref)]
    for q in range(TR // BLOCK):
        rows = slice(BLOCK * q, BLOCK * (q + 1))
        hot_ref[rows] = same_row(others, BLOCK * q, BLOCK)
        own_ref[rows] = same_row(own, BLOCK * q, BLOCK)


def cut_body(exps, *refs):
    packed_refs, hot_ref, (tile_ref, n1_ref, n2_ref, n3_ref) = refs[:exps], refs[exps], refs[exps + 1 :]
    share = PC // exps
    for k in range(exps):
        at = pl.multiple_of(share * met_group(exps, "join", k), share)
        tile_ref[pl.ds(at, share)] = packed_refs[k][...].astype(tile_ref.dtype)
    tile = tile_ref[...].astype(BF16)
    cut = dot(tile, hot_ref[...]).astype(BF16)
    head = tile[:, :PC].astype(F32).T[:PR].astype(BF16)
    n1_ref[0:PC] = cut[:, :PC]
    n1_ref[PC : PC + PR] = head
    n2_ref[0:PC] = cut[:, PC:]
    n2_ref[PC : PC + PR] = head
    n3_ref[...] = head


def template_body(tile_ref, hot_ref, out_ref, own_ref):
    for i in range(TR // PC):
        lanes = slice(PC * i, PC * (i + 1))
        out_ref[lanes] = tile_ref[:, lanes].astype(F32).T.astype(BF16)
    own_ref[...] = dot(tile_ref[...].astype(BF16), hot_ref[...]).astype(BF16)


def subtract_body(exps, matched_ref, own_ref, n1_ref, n2_ref, n3_ref, z_ref, out_ref):
    half = matched_ref.shape[0] // 2
    at = 4 * (PC // exps)
    meta = z_ref[at : at + PR].astype(F32)
    heads = [n1_ref[PC : PC + PR], n2_ref[PC : PC + PR], n3_ref[...]]
    heads.append(jnp.zeros((PC - REACH * PR, PC), BF16))
    heads = jnp.concatenate(heads, 0)
    row = iota((PC, PC), 0).astype(F32)
    middle = n1_ref[0:PC].astype(F32)
    for h, (ref, outer) in enumerate(((own_ref, 0.0), (n2_ref, 2.0))):
        hi, lo, step = meta_rows(meta, h)
        hot = jnp.where(row == spill_at(hi, lo, step), 1.0, 0.0).astype(BF16)
        back = jnp.where(step == outer, ref[0:PC].astype(F32), middle) + dot(heads, hot, 0, 0)
        back = back.T
        rows = slice(half * h, half * (h + 1))
        for c in range(2):
            lanes = slice(PC * c, PC * (c + 1))
            out_ref[rows, lanes] = (matched_ref[rows, lanes] - back[half * c : half * (c + 1)]).astype(BF16)


VM = pl.BlockSpec(memory_space=pltpu.VMEM)
HBM = pl.BlockSpec(memory_space=pltpu.HBM)


def call(body, outs, specs, scratch=(), micros=1):
    return pl.pallas_call(
        body,
        out_shape=tuple(jax.ShapeDtypeStruct(s, t) for s, t in outs),
        in_specs=specs,
        out_specs=tuple(VM for _ in outs),
        scratch_shapes=scratch,
        compiler_params=PARAMS,
        cost_estimate=pl.CostEstimate(
            flops=micros * 10**9, bytes_accessed=micros * 10**6, transcendentals=0
        ),
    )


def along_exp(x, i, exps, tiles, name):
    ways = [order[i] for order in partners(exps, name)]
    pairs = [(e * tiles + t, (e ^ ways[t % 2]) * tiles + t) for e in range(exps) for t in range(tiles)]
    return lax.ppermute(x, ("exp", "tile"), pairs)


def along_tile(x, by, tiles):
    return lax.ppermute(x, "tile", [(i, (i + by) % tiles) for i in range(tiles)])


def program_of(exps, tiles):
    def steps(science, mask_bits, variance, kernel_poly, basis_rows, basis_cols, destination, row_offset):
        height, across = science.shape[2:]
        share = PC // exps
        packs = BF16 if share % 16 == 0 else F32
        message = ((4 * share + PR, PC), BF16)
        args = (
            basis_rows, basis_cols, science.reshape(height, across),
            jnp.transpose(kernel_poly, (0, 3, 1, 2)), mask_bits.reshape(height, across),
            variance.reshape(height, across), destination.reshape(1, -1), row_offset.reshape(1, -1),
        )
        args = tuple(pltpu.with_memory_space_constraint(a, pltpu.HBM) for a in args)
        matched, *z = call(
            lambda *r: match_body(exps, tiles, *r),
            [((height, across), F32)] + [message] * exps,
            [HBM] * len(args),
            [(pltpu.SMEM if i == 3 else pltpu.VMEM)(a.shape, a.dtype) for i, a in enumerate(args)]
            + [pltpu.SemaphoreType.DMA((len(args),)), pltpu.VMEM((4, PC, PC), packs)],
        )(*args)
        z = [z[0]] + [along_exp(z[k], k, exps, tiles, "share") for k in range(1, exps)]
        big = ((2 * share * exps + PR * meta_tiles(exps) + PR, PC), BF16)
        m1, m2, m3 = call(lambda *r: pick_body(exps, *r), [big, big, ((PR, PC), BF16)], [VM] * exps)(*z)
        m1, m2, m3 = (along_tile(m, i + 1, tiles) for i, m in enumerate((m1, m2, m3)))
        (own,) = call(lambda *r: own_body(exps, *r), [((2 * share, TR), F32)], [VM] * exps)(*z)
        (far,) = call(lambda *r: far_body(exps, *r), [((2 * share, TR), F32)], [VM] * 2)(own, m2)
        (packed,) = call(lambda *r: sum_body(exps, *r), [((share, TR), BF16)], [VM] * 4)(far, m1, m2, m3)
        packed = [packed] + [along_exp(packed, k, exps, tiles, "join") for k in range(1, exps)]
        hot, own_hot = call(
            lambda *r: place_body(exps, *r), [((TR, 2 * PC), BF16), ((TR, PC), BF16)], [VM] * 3
        )(m1, m2, z[0])
        back = ((PC + PR, PC), BF16)
        tile, n1, n2, n3 = call(
            lambda *r: cut_body(exps, *r), [((PC, TR), packs), back, back, ((PR, PC), BF16)], [VM] * (exps + 1)
        )(*packed, hot)
        n1, n2, n3 = (along_tile(n, -1 - i, tiles) for i, n in enumerate((n1, n2, n3)))
        template, own = call(template_body, [((TR, PC), BF16), ((PC, PC), BF16)], [VM] * 2)(tile, own_hot)
        (difference,) = call(
            lambda *r: subtract_body(exps, *r), [((height, across), BF16)], [VM] * 6
        )(matched, own, n1, n2, n3, z[0])
        return template, difference[None, None]

    return steps


def solution(mesh):
    placed = (
        P("exp", "tile", None, None),
        P("exp", "tile", None, None),
        P("exp", "tile", None, None),
        P("exp", "tile", None, None),
        P(),
        P(),
        P("exp", "tile", None, None),
        P("exp", "tile", None),
    )
    return jax.shard_map(
        program_of(mesh.shape["exp"], mesh.shape["tile"]),
        mesh=mesh,
        in_specs=placed,
        out_specs=(P("tile", None), P("exp", "tile", None, None)),
        check_vma=False,
    )
```

```python
import jax
import jax.numpy as jnp
from jax import lax
from jax.experimental import pallas as pl
from jax.experimental.pallas import tpu as pltpu
from jax.sharding import PartitionSpec as P


PR = 16
PC = 128
TR = 1024
F32 = jnp.float32
BF16 = jnp.bfloat16
SENT = 32.0
REACH = 3
GRANT = 24 * 1024 * 1024
PARAMS = pltpu.CompilerParams(vmem_limit_bytes=GRANT)
PACKED = pltpu.CompilerParams(vmem_limit_bytes=GRANT)


def iota(shape, dim):
    return lax.broadcasted_iota(jnp.int32, shape, dim)


def dot(a, b, ca=1, cb=0):
    return lax.dot_general(a, b, (((ca,), (cb,)), ((), ())), preferred_element_type=F32)


def circulant(taps, reverse):
    count, ks = taps.shape
    half = ks // 2
    tap, lane = iota((ks, PC), 0), iota((ks, PC), 1)
    place = (half - tap) if reverse else (tap - half)
    pick = jnp.where((place + PC) % PC == lane, 1.0, 0.0).astype(BF16)
    row = dot(taps, pick)
    return [
        pltpu.roll(jnp.broadcast_to(row[b : b + 1], (PC, PC)), 0, 1, stride=1, stride_axis=0)
        for b in range(count)
    ]


def same_row(places, first, count):
    row = iota((count, PC), 0).astype(BF16)
    one, zero = jnp.ones((count, PC), BF16), jnp.zeros((count, PC), BF16)
    return jnp.concatenate(
        [jnp.where(row == (p - float(first)).astype(BF16), one, zero) for p in places], 1
    )


def meta_rows(meta, half):
    hi, lo, step = (meta[3 * half + i : 3 * half + i + 1] for i in range(3))
    return hi, lo, step


def spill_at(hi, lo, step):
    over = hi * 32.0 + lo - TR
    return jnp.where(over >= 0.0, over + PR * step, -1.0)


def meta_tiles(exps):
    return -(-2 * exps // PR)


def match_body(exps, tiles, *refs):
    args, matched_ref, z_refs = refs[:8], refs[8], refs[9 : 9 + exps]
    held, sems = refs[9 + exps : 17 + exps], refs[17 + exps]
    copies = [pltpu.make_async_copy(a, h, sems.at[i]) for i, (a, h) in enumerate(zip(args, held))]
    for copy in copies:
        copy.start()
    brow_ref, bcol_ref, sci_ref, poly_ref, mask_ref, var_ref, dest_ref, off_ref = held
    exp, tile = lax.axis_index("exp"), lax.axis_index("tile")
    height, across = sci_ref.shape
    bases = brow_ref.shape[0]
    copies[0].wait()
    copies[1].wait()
    d = iota((PC, PC), 1) - iota((PC, PC), 0)
    zero = jnp.zeros((PC, PC), F32)
    cols = circulant(bcol_ref[...], True)
    rows = circulant(brow_ref[...], False)
    for copy in copies[2:]:
        copy.wait()
    half = height // 2
    share = PC // exps
    pieces = dest_ref.shape[1]
    target, offset = dest_ref[...], off_ref[...]
    offset = jnp.where(target == tiles - 1, jnp.minimum(offset, TR - PR), offset)
    step = target - tile
    step = jnp.where(step < 0, step + tiles, step)
    known = jnp.concatenate(
        [(offset // 32).astype(F32), (offset % 32).astype(F32), step.astype(F32)]
        + [jnp.zeros((PR - 3, pieces), F32)],
        0,
    ).astype(BF16)
    piece, lane = iota((pieces, PC), 0), iota((pieces, PC), 1)
    per_half = half // PR
    sub = iota((PR, PC), 0)
    meta = jnp.zeros((PR, PC), F32)
    for h in range(2):
        under = 2 * (per_half * h + lane // PR % per_half) + lane // half
        spread = dot(known, jnp.where(piece == under, 1.0, 0.0).astype(BF16))
        pos = (spread[0:1] * 32.0 + spread[1:2]).astype(jnp.int32) + iota((1, PC), 1) % PR
        for i, v in enumerate(((pos // 32).astype(F32), (pos % 32).astype(F32), spread[2:3])):
            meta = jnp.where(sub == 3 * h + i, v, meta)
    meta = meta.astype(BF16)
    sci = sci_ref[...]
    y = (iota((height, 1), 0).astype(F32) - (height - 1) / 2.0) / (height / 2.0)
    x = (iota((1, across), 1).astype(F32) - (across - 1) / 2.0) / (across / 2.0)
    matched = jnp.zeros((height, across), F32)
    bands = []
    for b in range(bases):
        mid = jnp.where(jnp.abs(d) < PC // 2, cols[b], zero)
        up = jnp.where(d < -(PC // 2), cols[b], zero)
        low = jnp.where(d > PC // 2, cols[b], zero)
        bands.append(
            jnp.concatenate([jnp.concatenate([mid, up], 1), jnp.concatenate([low, mid], 1)], 0).astype(BF16)
        )
    first = dot(sci, jnp.concatenate(bands, 1)).astype(BF16)
    for b in range(bases):
        row_band = jnp.where(jnp.abs(d) < PC // 2, rows[b], zero).astype(BF16)
        second = dot(row_band, first[:, across * b : across * (b + 1)])
        along = jnp.broadcast_to(poly_ref[0, 0, 0, b] + poly_ref[0, 1, 0, b] * y, (height, across))
        matched += (along + poly_ref[0, 2, 0, b] * x) * second
    matched_ref[...] = matched
    rejected = jnp.bitwise_and(mask_ref[...], 7) != 0
    weight = jnp.where(rejected, 0.0, 1.0 / var_ref[...].astype(F32))
    weighted = matched * weight
    parts = refs[18 + exps]
    for h in range(2):
        for i, image in enumerate((weighted, weight)):
            rows_of = image[half * h : half * (h + 1)]
            stacked = jnp.concatenate([rows_of[:, :PC], rows_of[:, PC:]], 0)
            parts[2 * h + i] = stacked.T.astype(parts.dtype)
    for k in range(exps):
        at = pl.multiple_of(share * jnp.bitwise_xor(exp, k), share)
        for g in range(4):
            z_refs[k][share * g : share * (g + 1)] = parts[g, pl.ds(at, share)].astype(BF16)
        z_refs[k][4 * share : 4 * share + PR] = meta


def pick_body(exps, *refs):
    z_refs, (m1_ref, m2_ref, m3_ref) = refs[:exps], refs[exps:]
    share = PC // exps
    pair = 2 * share
    sub16 = iota((PR, PC), 0)
    spill_row = iota((REACH * PR, PC), 0).astype(F32)
    spill = jnp.zeros((REACH * PR, PC), F32)
    metas = [[jnp.zeros((PR, PC), F32) for _ in range(meta_tiles(exps))] for _ in range(2)]
    for k in range(exps):
        top, bottom = z_refs[k][0:pair], z_refs[k][pair : 2 * pair]
        meta = z_refs[k][2 * pair : 2 * pair + PR].astype(F32)
        (hi0, lo0, step0), (hi1, lo1, step1) = meta_rows(meta, 0), meta_rows(meta, 1)
        use_top = step0 == 1.0
        mixed = jnp.where(use_top, top.astype(F32), bottom.astype(F32)).astype(BF16)
        m1_ref[pair * k : pair * (k + 1)] = mixed
        m2_ref[pair * k : pair * (k + 1)] = bottom
        for data, at in ((top, spill_at(hi0, lo0, step0)), (bottom, spill_at(hi1, lo1, step1))):
            hot = jnp.where(spill_row == at, 1.0, 0.0).astype(BF16)
            spill += dot(hot, jnp.concatenate([data] * (PC // pair), 0), 1, 1)
        values = (
            (jnp.where(use_top, hi0, jnp.where(step1 == 1.0, hi1, -SENT)), jnp.where(use_top, lo0, lo1)),
            (jnp.where(step1 == 2.0, hi1, -SENT), lo1),
        )
        at, row = 2 * k // PR, 2 * k % PR
        for tiles_of, rows_of in zip(metas, values):
            for i, v in enumerate(rows_of):
                tiles_of[at] = jnp.where(sub16 == row + i, v, tiles_of[at])
    coarse = spill.astype(BF16)
    fine = (spill - coarse.astype(F32)).astype(BF16)
    both = jnp.where(
        iota((REACH * PR, PC), 1) < pair, coarse.astype(F32), fine.astype(F32)
    ).astype(BF16)
    base = pair * exps
    for s, (ref, tiles_of) in enumerate(((m1_ref, metas[0]), (m2_ref, metas[1]))):
        for i, m in enumerate(tiles_of):
            ref[base + PR * i : base + PR * (i + 1)] = m.astype(BF16)
        at = base + PR * len(tiles_of)
        ref[at : at + PR] = both[PR * s : PR * (s + 1)]
    m3_ref[...] = both[2 * PR :]


BLOCK = 256


def own_body(exps, *refs):
    z_refs, out_ref = refs[:exps], refs[exps]
    share = PC // exps
    pair = 2 * share
    data = jnp.concatenate([z[0:pair] for z in z_refs], 1)
    places = []
    for z in z_refs:
        hi, lo, step = meta_rows(z[2 * pair : 2 * pair + PR].astype(F32), 0)
        places.append(jnp.where(step == 0.0, hi * 32.0 + lo, -1.0))
    for q in range(TR // BLOCK):
        hot = same_row(places, BLOCK * q, BLOCK)
        out_ref[:, BLOCK * q : BLOCK * (q + 1)] = dot(data, hot, 1, 1)


def message_places(ref, exps, k):
    base = 2 * PC // exps * exps
    at, row = base + PR * (2 * k // PR), 2 * k % PR
    meta = ref[at : at + PR].astype(F32)
    return meta[row : row + 1] * 32.0 + meta[row + 1 : row + 2]


def message_sums(exps, prior_ref, ref, q):
    pair = 2 * PC // exps
    data = jnp.concatenate([ref[pair * k : pair * (k + 1)] for k in range(exps)], 1)
    places = [message_places(ref, exps, k) for k in range(exps)]
    lanes = slice(BLOCK * q, BLOCK * (q + 1))
    return dot(data, same_row(places, BLOCK * q, BLOCK), 1, 1) + prior_ref[:, lanes]


def far_body(exps, own_ref, m2_ref, out_ref):
    for q in range(TR // BLOCK):
        out_ref[:, BLOCK * q : BLOCK * (q + 1)] = message_sums(exps, own_ref, m2_ref, q)


def sum_body(exps, far_ref, m1_ref, m2_ref, m3_ref, out_ref):
    share = PC // exps
    pair = 2 * share
    at = pair * exps + PR * meta_tiles(exps)
    spill = m3_ref[...].astype(F32)
    for r in (m1_ref, m2_ref):
        spill += r[at : at + PR].astype(F32)
    spill += pltpu.roll(spill, PC - pair, 1)
    spill = jnp.concatenate([spill, jnp.zeros((PC - PR, PC), F32)], 0).T[:pair]
    for q in range(TR // BLOCK):
        total = message_sums(exps, far_ref, m1_ref, q)
        if q == 0:
            total = jnp.concatenate([total[:, :PC] + spill, total[:, PC:]], 1)
        lanes = slice(BLOCK * q, BLOCK * (q + 1))
        out_ref[:, lanes] = (total[:share] / jnp.maximum(total[share:], 1.0)).astype(BF16)


def place_body(exps, m1_ref, m2_ref, z_ref, hot_ref, own_ref):
    share = PC // exps
    hi, lo, step = meta_rows(z_ref[4 * share : 4 * share + PR].astype(F32), 0)
    own = [jnp.where(step == 0.0, hi * 32.0 + lo, -1.0)]
    others = [message_places(r, exps, 0) for r in (m1_ref, m2_ref)]
    for q in range(TR // BLOCK):
        rows = slice(BLOCK * q, BLOCK * (q + 1))
        hot_ref[rows] = same_row(others, BLOCK * q, BLOCK)
        own_ref[rows] = same_row(own, BLOCK * q, BLOCK)


def cut_body(exps, *refs):
    packed_refs, hot_ref, (tile_ref, n1_ref, n2_ref, n3_ref) = refs[:exps], refs[exps], refs[exps + 1 :]
    exp = lax.axis_index("exp")
    share = PC // exps
    for k in range(exps):
        at = pl.multiple_of(share * jnp.bitwise_xor(exp, k), share)
        tile_ref[pl.ds(at, share)] = packed_refs[k][...].astype(tile_ref.dtype)
    tile = tile_ref[...].astype(BF16)
    cut = dot(tile, hot_ref[...]).astype(BF16)
    head = tile[:, :PC].astype(F32).T[:PR].astype(BF16)
    n1_ref[0:PC] = cut[:, :PC]
    n1_ref[PC : PC + PR] = head
    n2_ref[0:PC] = cut[:, PC:]
    n2_ref[PC : PC + PR] = head
    n3_ref[...] = head


def template_body(tile_ref, hot_ref, out_ref, own_ref):
    for i in range(TR // PC):
        lanes = slice(PC * i, PC * (i + 1))
        out_ref[lanes] = tile_ref[:, lanes].astype(F32).T.astype(BF16)
    own_ref[...] = dot(tile_ref[...].astype(BF16), hot_ref[...]).astype(BF16)


def subtract_body(exps, matched_ref, own_ref, n1_ref, n2_ref, n3_ref, z_ref, out_ref):
    half = matched_ref.shape[0] // 2
    at = 4 * (PC // exps)
    meta = z_ref[at : at + PR].astype(F32)
    heads = [n1_ref[PC : PC + PR], n2_ref[PC : PC + PR], n3_ref[...]]
    heads.append(jnp.zeros((PC - REACH * PR, PC), BF16))
    heads = jnp.concatenate(heads, 0)
    row = iota((PC, PC), 0).astype(F32)
    middle = n1_ref[0:PC].astype(F32)
    for h, (ref, outer) in enumerate(((own_ref, 0.0), (n2_ref, 2.0))):
        hi, lo, step = meta_rows(meta, h)
        hot = jnp.where(row == spill_at(hi, lo, step), 1.0, 0.0).astype(BF16)
        back = jnp.where(step == outer, ref[0:PC].astype(F32), middle) + dot(heads, hot, 0, 0)
        back = back.T
        rows = slice(half * h, half * (h + 1))
        for c in range(2):
            lanes = slice(PC * c, PC * (c + 1))
            out_ref[rows, lanes] = (matched_ref[rows, lanes] - back[half * c : half * (c + 1)]).astype(BF16)


VM = pl.BlockSpec(memory_space=pltpu.VMEM)
HBM = pl.BlockSpec(memory_space=pltpu.HBM)


def call(body, outs, specs, name, scratch=(), micros=1):
    return pl.pallas_call(
        body,
        out_shape=tuple(jax.ShapeDtypeStruct(s, t) for s, t in outs),
        in_specs=specs,
        out_specs=tuple(VM for _ in outs),
        scratch_shapes=scratch,
        compiler_params=PACKED if name in ("own", "far", "sum") else PARAMS,
        cost_estimate=pl.CostEstimate(
            flops=micros * 10**9, bytes_accessed=micros * 10**6, transcendentals=0
        ),
    )


def along_exp(x, k, exps):
    return lax.ppermute(x, "exp", [(i, i ^ k) for i in range(exps)])


def along_tile(x, by, tiles):
    return lax.ppermute(x, "tile", [(i, (i + by) % tiles) for i in range(tiles)])


def program_of(exps, tiles):
    def steps(science, mask_bits, variance, kernel_poly, basis_rows, basis_cols, destination, row_offset):
        height, across = science.shape[2:]
        share = PC // exps
        packs = BF16 if share % 16 == 0 else F32
        message = ((4 * share + PR, PC), BF16)
        args = (
            basis_rows, basis_cols, science.reshape(height, across),
            jnp.transpose(kernel_poly, (0, 3, 1, 2)), mask_bits.reshape(height, across),
            variance.reshape(height, across), destination.reshape(1, -1), row_offset.reshape(1, -1),
        )
        args = tuple(pltpu.with_memory_space_constraint(a, pltpu.HBM) for a in args)
        matched, *z = call(
            lambda *r: match_body(exps, tiles, *r),
            [((height, across), F32)] + [message] * exps,
            [HBM] * len(args),
            "match",
            [(pltpu.SMEM if i == 3 else pltpu.VMEM)(a.shape, a.dtype) for i, a in enumerate(args)]
            + [pltpu.SemaphoreType.DMA((len(args),)), pltpu.VMEM((4, PC, PC), packs)],
        )(*args)
        z = [z[0]] + [along_exp(z[k], k, exps) for k in range(1, exps)]
        big = ((2 * share * exps + PR * meta_tiles(exps) + PR, PC), BF16)
        m1, m2, m3 = call(
            lambda *r: pick_body(exps, *r), [big, big, ((PR, PC), BF16)], [VM] * exps, "pick"
        )(*z)
        m1, m2, m3 = (along_tile(m, i + 1, tiles) for i, m in enumerate((m1, m2, m3)))
        (own,) = call(lambda *r: own_body(exps, *r), [((2 * share, TR), F32)], [VM] * exps, "own")(*z)
        (far,) = call(lambda *r: far_body(exps, *r), [((2 * share, TR), F32)], [VM] * 2, "far")(own, m2)
        (packed,) = call(
            lambda *r: sum_body(exps, *r), [((share, TR), BF16)], [VM] * 4, "sum"
        )(far, m1, m2, m3)
        packed = [packed] + [along_exp(packed, k, exps) for k in range(1, exps)]
        hot, own_hot = call(
            lambda *r: place_body(exps, *r), [((TR, 2 * PC), BF16), ((TR, PC), BF16)], [VM] * 3, "place"
        )(m1, m2, z[0])
        back = ((PC + PR, PC), BF16)
        tile, n1, n2, n3 = call(
            lambda *r: cut_body(exps, *r),
            [((PC, TR), packs), back, back, ((PR, PC), BF16)],
            [VM] * (exps + 1),
            "cut",
        )(*packed, hot)
        n1, n2, n3 = (along_tile(n, -1 - i, tiles) for i, n in enumerate((n1, n2, n3)))
        template, own = call(
            template_body, [((TR, PC), BF16), ((PC, PC), BF16)], [VM] * 2, "template"
        )(tile, own_hot)
        (difference,) = call(
            lambda *r: subtract_body(exps, *r), [((height, across), BF16)], [VM] * 6, "subtract"
        )(matched, own, n1, n2, n3, z[0])
        return template, difference[None, None]

    return steps


def solution(mesh):
    placed = (
        P("exp", "tile", None, None),
        P("exp", "tile", None, None),
        P("exp", "tile", None, None),
        P("exp", "tile", None, None),
        P(),
        P(),
        P("exp", "tile", None, None),
        P("exp", "tile", None),
    )
    return jax.shard_map(
        program_of(mesh.shape["exp"], mesh.shape["tile"]),
        mesh=mesh,
        in_specs=placed,
        out_specs=(P("tile", None), P("exp", "tile", None, None)),
        check_vma=False,
    )
```
